32 devices in a mesh: groups: 2 (over y), seq: 4 (over z), section: 2 (over x), head: 2 (over core).
Axes of the slice: x: 2, y: 2, z: 4, core: 2. Of those that a mesh axis runs over, the one named last changes fastest.
Arguments:
- queries: bfloat16 [64, 64, 128], P(('groups', 'seq'), ('section', 'head')), parts along dimension 0, may hold values from -56 to 56
- key_cache: bfloat16 [15872, 8, 128], P(('groups', 'seq'), ('section', 'head')), parts along dimension 0, may hold values from -5 to 5
- value_cache: bfloat16 [15872, 8, 128], P(('groups', 'seq'), ('section', 'head')), parts along dimension 0, may hold values from -5 to 5
- new_features: bfloat16 [512, 8192], P(('groups', 'seq')), parts along dimension 0, may hold values from -60 to 60
- key_weight: bfloat16 [8192, 1024], P('seq', ('section', 'head')), may hold values from -2 to 2
- value_weight: bfloat16 [8192, 1024], P('seq', ('section', 'head')), may hold values from -0.0625 to 0.0625
- key_gain: float32 [128], replicated, may hold values from 0.5 to 2
- out_weight: bfloat16 [8192, 8192], P(('section', 'head'), 'seq'), may hold values from -0.5 to 0.5
- frame_length: int32 [128], P('groups'), parts along dimension 0, may hold values from 1 to 256, 8192 in all
- text_frame: int32 [64], P(('groups', 'seq')), parts along dimension 0, may hold values from 0 to 63
Outputs:
- layer_output: bfloat16 [64, 8192], P(('groups', 'section', 'head'), 'seq'), parts along dimension 0
- new_keys: bfloat16 [512, 8, 128], P(('groups', 'seq'), ('section', 'head')), parts along dimension 0
- new_values: bfloat16 [512, 8, 128], P(('groups', 'seq'), ('section', 'head')), parts along dimension 0
The draws below stay inside these ranges and needn't reach their ends.
There are 2 independent parts, one for each index of `groups`. The reference program is written for one: setup_inputs(seed, part) draws one part's arguments, and reference() takes and returns one part's arrays. A program takes and returns all parts, laid end to end along the dimension named above; an argument that names none is the same for every part. Nothing has to cross between parts.
Inputs may be any that keep to these rules, and one draw needn't show every extreme that they name: `frame_length`: they sum to 8192.
All inputs are finite; a program needn't handle non-finite values.
Results may differ from the reference program's by a relative error of at most 0.015.
Values may be sent and summed in bfloat16 or wider, within the bound.
No kernel may reach another device: no remote copies, remote signals or barrier semaphores. Data moves between devices by JAX's collectives and lax.ppermute only.
A program may use at most 64 MiB of HBM per device.

```python
import math
import jax
import jax.numpy as jnp
import numpy as np
from jax import lax

D = 8192
HQ = 64
KVH = 8
HD = 128
RES_DEV = 1984
NEW_DEV = 64
FRAMES = 64
GROUP = 8
TEXT = 32
RES = 7936
NEW = 256
VTOK = 8192
FRAME_MOST = 256
N_SEQ = 4


def cache_sample(key):
    sample = jnp.clip(jax.random.normal(jax.random.fold_in(key, 101), (RES, KVH, HD), jnp.float32), -5.0, 5.0)
    return sample


def draw_key_cache(key, part):
    return cache_sample(key).astype(jnp.bfloat16)


def draw_queries(key, part):
    sample = jnp.clip(jax.random.normal(jax.random.fold_in(key, 201), (TEXT, HQ, HD), jnp.float32), -5.0, 5.0)
    return sample.astype(jnp.bfloat16)


def draw_new_features(key, part):
    row_scale = jnp.exp(jax.random.uniform(jax.random.fold_in(key, 301), (NEW, 1), jnp.float32, 0.0, math.log(10.0)))
    sample = jnp.clip(jax.random.normal(jax.random.fold_in(key, 302), (NEW, D), jnp.float32), -5.0, 5.0)
    return (sample * row_scale).astype(jnp.bfloat16)


def draw_key_weight(key, part):
    col_scale = jnp.exp(jax.random.uniform(jax.random.fold_in(key, 401), (1, KVH * HD), jnp.float32, math.log(0.3), math.log(3.0)))
    sample = jnp.clip(jax.random.normal(jax.random.fold_in(key, 402), (D, KVH * HD), jnp.float32), -5.0, 5.0)
    return (sample * col_scale * D ** (-0.5)).astype(jnp.bfloat16)


def set_ends(entries, own_key, least, largest):
    index_at = [jax.random.randint(jax.random.fold_in(own_key, axis), (), 0, length) for axis, length in enumerate(entries.shape)]
    longest = entries.shape.index(max(entries.shape))
    next_to = index_at[:longest] + [(index_at[longest] + 1) % entries.shape[longest]] + index_at[longest + 1:]
    return entries.at[tuple(index_at)].set(least).at[tuple(next_to)].set(largest)


def block_scale(own_key, extent, pieces, low, largest):
    factor_of, own = 1.0, jax.random.fold_in(own_key, 6)
    for axis_at, blocks in pieces:
        steps = jnp.exp(jax.random.uniform(jax.random.fold_in(own, axis_at), (blocks,), jnp.float32, low / len(pieces), largest / len(pieces)))
        factor_of = factor_of * jnp.repeat(steps, extent[axis_at] // blocks).reshape([-1 if axis == axis_at else 1 for axis in range(len(extent))])
    return factor_of


def length_profile(amount, total, most, lean):
    weights = [(1 << 20) // math.isqrt(grade ** lean) + 1 for grade in range(2, amount + 1)]
    rest, holding = total - most - (amount - 1), [1] * (amount - 1)
    while rest > 0:
        movable = [i for i in range(amount - 1) if holding[i] < most]
        mass, left = sum([weights[i] for i in movable]), rest
        for i in movable:
            extra = min(most - holding[i], max(1, left * weights[i] // mass), rest)
            holding[i] = holding[i] + extra
            rest = rest - extra
    return np.array([most] + holding)


def ragged(own_key, amount, total, most, lean):
    if amount == 2:
        one = jax.random.randint(own_key, (), max(1, total - most), min(most, total - 1) + 1)
        return jnp.stack([one, total - one])
    tallies = jnp.asarray(length_profile(amount, total, most, lean), jnp.int32)
    couples = (amount - 1) // 2
    donor, taker = tallies[1:1 + 2 * couples:2], tallies[2:2 + 2 * couples:2]
    room = jnp.minimum(donor - 1, most - taker)
    passed = jax.random.randint(jax.random.fold_in(own_key, 1), (couples,), 0, 1 << 20) % (room + 1)
    tallies = tallies.at[1:1 + 2 * couples:2].set(donor - passed).at[2:2 + 2 * couples:2].set(taker + passed)
    return tallies[jax.random.permutation(jax.random.fold_in(own_key, 2), amount)]


def scatter_about(stream_key, extent, deviation, reach, pieces=(), kind=jnp.bfloat16):
    result = deviation * jax.random.normal(stream_key, extent, jnp.float32)
    if pieces:
        result = result * block_scale(stream_key, extent, pieces, -0.22, 0.18)
    return jnp.clip(result, -reach, reach).astype(kind)


def setup_inputs(seed: int = 0, part: int = 0) -> dict:
    keys = jax.random.split(jax.random.key(seed), 11)
    part_keys = jax.random.split(jax.random.fold_in(keys[10], part), 11)
    return {
        "queries": draw_queries(jax.random.fold_in(jax.random.fold_in(keys[10], part), 71), part),
        "key_cache": draw_key_cache(jax.random.fold_in(jax.random.fold_in(keys[10], part), 71), part),
        "value_cache": scatter_about(part_keys[2], (RES, KVH, HD), 1.0, 5.0, ((0, 4), (1, 4))),
        "new_features": draw_new_features(jax.random.fold_in(jax.random.fold_in(keys[10], part), 71), part),
        "key_weight": draw_key_weight(jax.random.fold_in(keys[10], 71), part),
        "value_weight": scatter_about(keys[5], (D, KVH * HD), D ** -0.5, 0.0625, ((0, 4), (1, 4))),
        "key_gain": jnp.clip(jnp.exp(jax.random.uniform(keys[6], (HD,), jnp.float32, math.log(0.5), math.log(2.0))), 0.5, 2.0),
        "out_weight": scatter_about(keys[7], (HQ * HD, D), (HQ * HD // 64) ** -0.5, 0.5, ((0, 4), (1, 4))),
        "frame_length": ragged(part_keys[8], FRAMES, VTOK, FRAME_MOST, 1).astype(jnp.int32),
        "text_frame": set_ends(jax.random.randint(part_keys[9], (TEXT,), 0, FRAMES), jax.random.fold_in(part_keys[9], 1), 0, FRAMES - 1).astype(jnp.int32),
    }


masked_score = -1e+30
norm_epsilon = 1e-05

def reference(queries, key_cache, value_cache, new_features, key_weight, value_weight, key_gain, out_weight, frame_length, text_frame):
    key_raw = jnp.dot(new_features, key_weight, preferred_element_type=jnp.float32)
    value_raw = jnp.dot(new_features, value_weight, preferred_element_type=jnp.float32)
    key_heads = key_raw.reshape(NEW, KVH, HD)
    mean_square = lax.optimization_barrier(jnp.mean(key_heads * key_heads, axis=2, keepdims=True))
    new_keys = (key_heads * lax.rsqrt(mean_square + norm_epsilon) * key_gain).astype(jnp.bfloat16)
    new_values = value_raw.reshape(NEW, KVH, HD).astype(jnp.bfloat16)
    all_keys = jnp.concatenate((key_cache.reshape(N_SEQ, RES_DEV, KVH, HD), new_keys.reshape(N_SEQ, NEW_DEV, KVH, HD)), axis=1).reshape(VTOK, KVH, HD)
    all_values = jnp.concatenate((value_cache.reshape(N_SEQ, RES_DEV, KVH, HD), new_values.reshape(N_SEQ, NEW_DEV, KVH, HD)), axis=1).reshape(VTOK, KVH, HD)
    frame_ends = jnp.cumsum(frame_length).astype(jnp.int32)
    row_limit = frame_ends[text_frame.astype(jnp.int32)]
    positions = jnp.arange(VTOK, dtype=jnp.int32)
    visible = positions[None, :] < row_limit[:, None]
    score_scale = HD ** (-0.5)

    def head_result(head_index):
        query_rows = lax.dynamic_index_in_dim(queries, head_index, 1, keepdims=False)
        kv_index = head_index // GROUP
        head_keys = lax.dynamic_index_in_dim(all_keys, kv_index, 1, keepdims=False)
        head_values = lax.dynamic_index_in_dim(all_values, kv_index, 1, keepdims=False)
        scores = jnp.dot(query_rows, head_keys.T, preferred_element_type=jnp.float32) * score_scale
        row_peak = lax.optimization_barrier(jnp.max(jnp.where(visible, scores, masked_score), axis=1))
        weights = jnp.where(visible, jnp.exp(scores - row_peak[:, None]), 0.0)
        row_total = lax.optimization_barrier(jnp.sum(weights, axis=1))
        summed_rows = jnp.dot(weights.astype(jnp.bfloat16), head_values, preferred_element_type=jnp.float32)
        return (summed_rows / row_total[:, None]).astype(jnp.bfloat16)
    attended = lax.map(head_result, jnp.arange(HQ, dtype=jnp.int32))
    attended = jnp.transpose(attended, (1, 0, 2)).reshape(TEXT, HQ * HD)
    layer_output = jnp.dot(attended, out_weight, preferred_element_type=jnp.float32).astype(jnp.bfloat16)
    return (layer_output, new_keys, new_values)
```

```python
import jax
import jax.numpy as jnp
from jax import lax
from jax.sharding import PartitionSpec as P

masked_score = -1e30
norm_epsilon = 1e-05


def shifted(part, axis, by):
    peers = lax.axis_size(axis)
    return lax.ppermute(part, axis, [(i, (i + by) % peers) for i in range(peers)])


def block_at(array, index, axis=0):
    return lax.dynamic_index_in_dim(array, index, axis, keepdims=False)


def gathered(part, axis):
    peers = lax.axis_size(axis)
    return [part] + [shifted(part, axis, by) for by in range(1, peers)]


def summed_rows(partial, axis, dtype):
    peers = lax.axis_size(axis)
    me = lax.axis_index(axis)
    total = block_at(partial, me).astype(jnp.float32)
    for by in range(1, peers):
        piece = block_at(partial, (me + by) % peers).astype(dtype)
        total = total + shifted(piece, axis, by).astype(jnp.float32)
    return total


def split_three(value):
    high = lax.reduce_precision(value, 8, 7)
    rest = value - high
    middle = lax.reduce_precision(rest, 8, 7)
    low = rest - middle
    return [piece.astype(jnp.bfloat16) for piece in (high, middle, low)]


def attend_block(grouped, key_block, value_block, key_position, row_limit, score_scale):
    scores = (
        jnp.einsum("rcgd,kcd->rcgk", grouped, key_block, preferred_element_type=jnp.float32)
        * score_scale
    )
    visible = (key_position[None, :] < row_limit[:, None])[:, None, None, :]
    peak = jnp.max(jnp.where(visible, scores, masked_score), axis=3)
    weights = jnp.where(visible, jnp.exp(scores - peak[..., None]), 0.0)
    total = jnp.sum(weights, axis=3)
    update = jnp.einsum(
        "rcgk,kcd->rcgd",
        weights.astype(jnp.bfloat16),
        value_block,
        preferred_element_type=jnp.float32,
    )
    return update, peak, total


def on_device(
    queries,
    key_cache,
    value_cache,
    new_features,
    key_weight,
    value_weight,
    key_gain,
    out_weight,
    frame_length,
    text_frame,
):
    head_depth = key_cache.shape[2]
    local_kv = key_cache.shape[1]
    kv_width = key_weight.shape[1]
    cached_rows = key_cache.shape[0]
    new_rows = new_features.shape[0]
    text_rows, local_heads, _ = queries.shape
    group_size = local_heads // local_kv
    seq_size = lax.axis_size("seq")
    head_size = lax.axis_size("head")
    seq_index = lax.axis_index("seq")
    head_index = lax.axis_index("head")
    bf16 = jnp.bfloat16
    f32 = jnp.float32

    frame_index = jnp.arange(frame_length.shape[0], dtype=jnp.int32)
    row_limit = jnp.sum(
        jnp.where(frame_index[None, :] <= text_frame[:, None], frame_length[None, :], 0), axis=1
    )

    digits = jnp.stack([row_limit % 256, (row_limit // 256) % 256, row_limit // 65536])
    digits = jnp.pad(digits.astype(bf16), ((0, 0), (0, head_depth - text_rows)))
    query_message = jnp.concatenate(
        (queries.reshape(text_rows * local_heads, head_depth), digits), axis=0
    )

    half_rows = new_rows // head_size
    depth = key_weight.shape[0]
    feature_blocks = new_features.reshape(head_size, half_rows, seq_size, depth)
    my_half = block_at(feature_blocks, head_index)
    sent_features = []
    for by in range(1, seq_size):
        piece = block_at(my_half, (seq_index + by) % seq_size, 1)
        sent_features.append(piece)

    query_messages = gathered(query_message, "seq")
    arrived = [shifted(piece, "seq", by + 1) for by, piece in enumerate(sent_features)]
    stacked_weight = jnp.concatenate((key_weight, value_weight), axis=1)

    own_chunk = block_at(feature_blocks, seq_index, 2)
    own_rows = [block_at(own_chunk, (head_index + by) % head_size) for by in range(head_size)]
    own_rows = jnp.concatenate(own_rows, axis=0)
    raw = jnp.dot(own_rows, stacked_weight, preferred_element_type=f32)
    for by, half in enumerate(arrived):
        whole = jnp.concatenate(
            [half] + [shifted(half, "head", head_size - turn) for turn in range(1, head_size)],
            axis=0,
        )
        term = jnp.dot(whole, stacked_weight, preferred_element_type=f32).astype(bf16)
        raw = raw + shifted(term, "seq", seq_size - (by + 1)).astype(f32)
    raw = raw.reshape(head_size, half_rows, -1)
    raw = jnp.concatenate(
        [block_at(raw, (turn - head_index) % head_size) for turn in range(head_size)], axis=0
    )

    stacked_query = jnp.stack([m[: text_rows * local_heads] for m in query_messages])
    stacked_digit = jnp.stack([m[text_rows * local_heads :, :text_rows] for m in query_messages])
    stacked_digit = stacked_digit.astype(f32)
    limits = stacked_digit[:, 0] + 256.0 * stacked_digit[:, 1] + 65536.0 * stacked_digit[:, 2]
    grouped = stacked_query.reshape(seq_size, text_rows, local_kv, group_size, head_depth)
    score_scale = head_depth ** (-0.5)
    block_keys = cached_rows + new_rows
    key_position = (seq_index * block_keys + jnp.arange(block_keys, dtype=jnp.int32)).astype(f32)

    many = 4
    part_count = seq_size // many if seq_size > many else 1
    part_rows = seq_size // part_count * text_rows
    grouped = grouped.reshape(part_count, part_rows, local_kv, group_size, head_depth)
    limits = limits.reshape(part_count, part_rows)

    def cached_part(operands):
        query_part, limit_part = operands
        return attend_block(
            query_part, key_cache, value_cache, key_position[:cached_rows], limit_part, score_scale
        )

    if part_count == 1:
        cached = cached_part((grouped[0], limits[0]))
    else:
        cached = lax.map(cached_part, (grouped, limits))
    grouped = grouped.reshape(-1, local_kv, group_size, head_depth)
    limits = limits.reshape(-1)
    cached_sum, cached_peak, cached_total = (
        part.reshape(grouped.shape[0], local_kv, group_size, *part.shape[part.ndim - (1 if i == 0 else 0) :])
        for i, part in enumerate(cached)
    )

    key_heads = raw[:, :kv_width].reshape(new_rows, local_kv, head_depth)
    mean_square = jnp.mean(key_heads * key_heads, axis=2, keepdims=True)
    new_keys = (key_heads * lax.rsqrt(mean_square + norm_epsilon) * key_gain).astype(bf16)
    new_values = raw[:, kv_width:].reshape(new_rows, local_kv, head_depth).astype(bf16)
    fresh_sum, fresh_peak, fresh_total = attend_block(
        grouped, new_keys, new_values, key_position[cached_rows:], limits, score_scale
    )
    peak = jnp.maximum(cached_peak, fresh_peak)
    cached_factor = jnp.exp(cached_peak - peak)
    fresh_factor = jnp.exp(fresh_peak - peak)
    total = cached_factor * cached_total + fresh_factor * fresh_total
    summed = cached_factor[..., None] * cached_sum + fresh_factor[..., None] * fresh_sum
    some = total > 0.0
    safe_total = jnp.where(some, total, 1.0)
    mean_value = (summed / safe_total[..., None]).astype(bf16)
    log_total = jnp.where(some, peak + jnp.log(safe_total), masked_score)

    mean_value = mean_value.reshape(seq_size, text_rows * local_heads, head_depth)
    log_total = log_total.reshape(seq_size, text_rows * local_heads)
    log_count = text_rows * local_heads
    log_rows = -(-log_count // head_depth)
    log_pieces = jnp.stack(split_three(log_total), axis=1)
    log_pieces = jnp.pad(log_pieces, ((0, 0), (0, 0), (0, log_rows * head_depth - log_count)))
    log_pieces = log_pieces.reshape(seq_size, 3 * log_rows, head_depth)
    message = jnp.concatenate((mean_value, log_pieces), axis=1)
    returned = [message[0]] + [
        shifted(message[by], "seq", seq_size - by) for by in range(1, seq_size)
    ]
    returned = jnp.stack(returned)
    means = returned[:, : text_rows * local_heads].astype(f32)
    logs = returned[:, text_rows * local_heads :].astype(f32)
    logs = jnp.sum(logs.reshape(seq_size, 3, -1), axis=1)[:, :log_count]
    top = jnp.max(logs, axis=0)
    share = jnp.exp(logs - top[None])
    merged = jnp.sum(share[..., None] * means, axis=0) / jnp.sum(share, axis=0)[:, None]
    attended = merged.astype(bf16).reshape(text_rows, local_heads * head_depth)

    every = jnp.stack(gathered(attended, "seq"))
    order = (seq_index - jnp.arange(seq_size)) % seq_size
    every = jnp.concatenate([block_at(every, order[i]) for i in range(seq_size)], axis=0)
    partial = jnp.dot(every, out_weight, preferred_element_type=f32)

    section_size = lax.axis_size("section")
    out_rows = partial.shape[0] // (section_size * head_size)
    partial = partial.reshape(section_size, head_size, out_rows, -1)
    partial = summed_rows(jnp.swapaxes(partial, 0, 1), "head", bf16)
    layer_output = summed_rows(partial, "section", bf16).astype(bf16)
    return (layer_output, new_keys, new_values)


def solution(mesh):
    placed = (
        P(("groups", "seq"), ("section", "head"), None),
        P(("groups", "seq"), ("section", "head"), None),
        P(("groups", "seq"), ("section", "head"), None),
        P(("groups", "seq"), None),
        P("seq", ("section", "head")),
        P("seq", ("section", "head")),
        P(),
        P(("section", "head"), "seq"),
        P("groups"),
        P(("groups", "seq")),
    )
    return jax.shard_map(
        on_device,
        mesh=mesh,
        in_specs=placed,
        out_specs=(
            P(("groups", "section", "head"), "seq"),
            P(("groups", "seq"), ("section", "head"), None),
            P(("groups", "seq"), ("section", "head"), None),
        ),
        check_vma=False,
    )
```

```python
import functools

import jax
import jax.numpy as jnp
from jax import lax
from jax.experimental import pallas as pl
from jax.experimental.pallas import tpu as pltpu
from jax.sharding import PartitionSpec as P

masked_score = -1e30
norm_epsilon = 1e-05
bf16 = jnp.bfloat16
f32 = jnp.float32


def shifted(part, axis, by):
    peers = lax.axis_size(axis)
    return lax.ppermute(part, axis, [(i, (i + by) % peers) for i in range(peers)])


def block_at(array, index, axis=0):
    return lax.dynamic_index_in_dim(array, index, axis, keepdims=False)


def summed_rows(partial, axis):
    peers = lax.axis_size(axis)
    me = lax.axis_index(axis)
    total = block_at(partial, me)
    for by in range(1, peers):
        piece = block_at(partial, (me + by) % peers).astype(bf16)
        total = total + shifted(piece, axis, by).astype(f32)
    return total


vmem = pl.BlockSpec(memory_space=pltpu.VMEM)
smem = pl.BlockSpec(memory_space=pltpu.SMEM)


def call(body, outs, name, flops, moved, n_scalar, n_in, scratch=(), limit=None):
    return pl.pallas_call(
        body,
        out_shape=outs,
        in_specs=[smem] * n_scalar + [vmem] * n_in,
        out_specs=jax.tree.map(lambda _: vmem, outs),
        scratch_shapes=list(scratch),
        name=name,
        cost_estimate=pl.CostEstimate(flops=flops, bytes_accessed=moved, transcendentals=0),
        compiler_params=pltpu.CompilerParams(vmem_limit_bytes=limit or (16 << 20)),
    )


def project_body(halves, *refs):
    row_refs, (key_ref, value_ref, out_ref) = refs[:halves], refs[halves:]
    rows = jnp.concatenate([ref[...] for ref in row_refs], axis=0)
    width = key_ref.shape[1]
    out_ref[:, :width] = jnp.dot(rows, key_ref[...], preferred_element_type=f32).astype(out_ref.dtype)
    out_ref[:, width:] = jnp.dot(rows, value_ref[...], preferred_element_type=f32).astype(out_ref.dtype)


def row_limits(message_refs, unit_rows, query_rows):
    columns = []
    for ref in message_refs:
        digits = ref[query_rows:, :].astype(f32)
        limit = digits[:unit_rows, 0:1] + 256.0 * digits[:unit_rows, 1:2] + 65536.0 * digits[:unit_rows, 2:3]
        columns.append(limit)
    return columns


def cached_body(blocks, text_rows, kv, scale, *refs):
    base_ref = refs[0]
    message_refs = refs[1 : 1 + blocks]
    key_ref, value_ref, sum_ref, peak_ref, total_ref = refs[1 + blocks :]
    depth = message_refs[0].shape[1]
    query_rows = message_refs[0].shape[0] - 16
    unit = query_rows // kv
    group = unit // text_rows
    keys = key_ref.shape[0]
    base = base_ref[0]
    step = min(blocks, 4)
    position = lax.broadcasted_iota(jnp.int32, (step * unit, keys), 1) + base
    for start in range(0, blocks, step):
        some = message_refs[start : start + step]
        limit = jnp.concatenate(
            [jnp.concatenate([c] * group, axis=0) for c in row_limits(some, text_rows, query_rows)],
            axis=0,
        )
        visible = position < limit.astype(jnp.int32)
        for c in range(kv):
            query = jnp.concatenate([ref[c * unit : (c + 1) * unit, :] for ref in some], axis=0)
            lanes = slice(c * depth, (c + 1) * depth)
            scores = lax.dot_general(
                query, key_ref[:, lanes], (((1,), (1,)), ((), ())), preferred_element_type=f32
            ) * scale
            scores = jnp.where(visible, scores, masked_score)
            peak = jnp.max(scores, axis=1, keepdims=True)
            weights = jnp.where(visible, jnp.exp(scores - peak), 0.0)
            total = jnp.sum(weights, axis=1, keepdims=True)
            summed = jnp.dot(weights.astype(bf16), value_ref[:, lanes], preferred_element_type=f32)
            rows = slice(start * unit, (start + step) * unit)
            sum_ref[c, rows, :] = summed
            peak_ref[c, rows, :] = jnp.broadcast_to(peak, summed.shape)
            total_ref[c, rows, :] = jnp.broadcast_to(total, summed.shape)


def fresh_body(blocks, text_rows, kv, halves, scale, *refs):
    base_ref, half_ref = refs[:2]
    message_refs = refs[2 : 2 + blocks]
    own_ref = refs[2 + blocks]
    term_refs = refs[3 + blocks : 2 + 2 * blocks]
    gain_ref, sum_ref, peak_ref, total_ref, key_out, value_out = refs[2 + 2 * blocks : 8 + 2 * blocks]
    out_refs = refs[8 + 2 * blocks :]
    depth = message_refs[0].shape[1]
    query_rows = message_refs[0].shape[0] - 16
    unit = query_rows // kv
    group = unit // text_rows
    width = kv * depth
    raw = term_refs[0][...].astype(f32)
    for ref in term_refs[1:]:
        raw = raw + ref[...].astype(f32)
    count = raw.shape[0] // halves
    my_half = half_ref[0]
    turned = raw
    for turn in range(1, halves):
        other = jnp.concatenate((raw[-turn * count :], raw[: -turn * count]), axis=0)
        turned = jnp.where(my_half == turn, other, turned)
    raw = turned + own_ref[...]
    keys = raw.shape[0]
    value_rows = raw[:, width:].astype(bf16)
    value_out[...] = value_rows
    position = lax.broadcasted_iota(jnp.int32, (unit, keys), 1) + base_ref[0]
    limits = [
        jnp.concatenate([c] * group, axis=0).astype(jnp.int32)
        for c in row_limits(message_refs, text_rows, query_rows)
    ]
    diagonal = lax.broadcasted_iota(jnp.int32, (unit, unit), 0) == lax.broadcasted_iota(
        jnp.int32, (unit, unit), 1
    )
    key_rows = []
    for c in range(kv):
        lanes = slice(c * depth, (c + 1) * depth)
        part = raw[:, lanes]
        mean_square = jnp.mean(part * part, axis=1, keepdims=True)
        normed = (part * lax.rsqrt(mean_square + norm_epsilon) * gain_ref[...]).astype(bf16)
        key_out[:, lanes] = normed
        key_rows.append(normed)
    for at in range(blocks):
        visible = position < limits[at]
        logs = []
        for c in range(kv):
            lanes = slice(c * depth, (c + 1) * depth)
            query = message_refs[at][c * unit : (c + 1) * unit, :]
            scores = lax.dot_general(
                query, key_rows[c], (((1,), (1,)), ((), ())), preferred_element_type=f32
            ) * scale
            scores = jnp.where(visible, scores, masked_score)
            rows = slice(at * unit, (at + 1) * unit)
            old_peak = peak_ref[c, rows, :]
            peak = jnp.maximum(jnp.max(scores, axis=1, keepdims=True), old_peak)
            weights = jnp.where(visible, jnp.exp(scores - peak[:, :1]), 0.0)
            factor = jnp.exp(old_peak - peak)
            total = factor * total_ref[c, rows, :] + jnp.sum(weights, axis=1, keepdims=True)
            summed = factor * sum_ref[c, rows, :] + jnp.dot(
                weights.astype(bf16), value_rows[:, lanes], preferred_element_type=f32
            )
            some = total > 0.0
            safe = jnp.where(some, total, 1.0)
            out_refs[at][c * unit : (c + 1) * unit, :] = (summed / safe).astype(bf16)
            log = jnp.where(some, peak + jnp.log(safe), masked_score)
            logs.append(jnp.sum(jnp.where(diagonal, log[:, :1], 0.0), axis=0, keepdims=True))
        log = jnp.concatenate(logs, axis=1)
        if log.shape[1] < depth:
            log = jnp.concatenate((log, jnp.zeros((1, depth - log.shape[1]), f32)), axis=1)
        high = log.astype(bf16).astype(f32)
        middle = (log - high).astype(bf16).astype(f32)
        low = log - high - middle
        pieces = jnp.concatenate((high, middle, low, jnp.zeros((13, depth), f32)), axis=0)
        out_refs[at][query_rows:, :] = pieces.astype(bf16)


def merge_body(blocks, text_rows, *refs):
    message_refs, out_ref = refs[:blocks], refs[blocks]
    depth = message_refs[0].shape[1]
    query_rows = message_refs[0].shape[0] - 16
    logs = []
    diagonal = lax.broadcasted_iota(jnp.int32, (depth, depth), 0) == lax.broadcasted_iota(
        jnp.int32, (depth, depth), 1
    )
    for ref in message_refs:
        pieces = ref[query_rows:, :].astype(f32)
        logs.append(pieces[0:1] + pieces[1:2] + pieces[2:3])
    top = logs[0]
    for log in logs[1:]:
        top = jnp.maximum(top, log)
    shares = [jnp.exp(log - top) for log in logs]
    whole = shares[0]
    for share in shares[1:]:
        whole = whole + share
    merged = None
    for share, ref in zip(shares, message_refs):
        column = jnp.sum(jnp.where(diagonal, share / whole, 0.0), axis=1, keepdims=True)
        term = column[:query_rows] * ref[:query_rows, :].astype(f32)
        merged = term if merged is None else merged + term
    for head in range(query_rows // text_rows):
        out_ref[:, head * depth : (head + 1) * depth] = merged[
            head * text_rows : (head + 1) * text_rows
        ].astype(bf16)


def output_body(blocks, *refs):
    index_ref = refs[0]
    row_refs = refs[1 : 1 + blocks]
    weight_ref, out_ref, rows_ref = refs[1 + blocks :]
    count = row_refs[0].shape[0]
    for by, ref in enumerate(row_refs):
        at = lax.rem(index_ref[0] + (blocks - by), blocks)
        rows_ref[pl.ds(pl.multiple_of(at * count, count), count), :] = ref[...].astype(f32)
    rows = rows_ref[...].astype(bf16)
    out_ref[...] = jnp.dot(rows, weight_ref[...], preferred_element_type=f32)


def on_device(
    queries,
    key_cache,
    value_cache,
    new_features,
    key_weight,
    value_weight,
    key_gain,
    out_weight,
    frame_length,
    text_frame,
):
    cached_rows, local_kv, head_depth = key_cache.shape
    kv_width = key_weight.shape[1]
    depth = key_weight.shape[0]
    new_rows = new_features.shape[0]
    text_rows, local_heads, _ = queries.shape
    group = local_heads // local_kv
    query_rows = text_rows * local_heads
    seq_size = lax.axis_size("seq")
    head_size = lax.axis_size("head")
    section_size = lax.axis_size("section")
    seq_index = lax.axis_index("seq")
    head_index = lax.axis_index("head")
    half_rows = new_rows // head_size
    sds = jax.ShapeDtypeStruct

    arrived = []
    for by in range(1, seq_size):
        at = (seq_index + by) % seq_size
        piece = lax.dynamic_slice(
            new_features, (head_index * half_rows, at * depth), (half_rows, depth)
        )
        arrived.append(shifted(piece, "seq", by))
    own_rows = lax.dynamic_slice(new_features, (0, seq_index * depth), (new_rows, depth))

    frame_index = jnp.arange(frame_length.shape[0], dtype=jnp.int32)
    row_limit = jnp.sum(
        jnp.where(frame_index[None, :] <= text_frame[:, None], frame_length[None, :], 0), axis=1
    )
    digits = jnp.stack([row_limit % 256, (row_limit // 256) % 256, row_limit // 65536], axis=1)
    digits = jnp.pad(digits.astype(bf16), ((0, 16 - text_rows), (0, head_depth - 3)))
    grouped = queries.reshape(text_rows, local_kv, group, head_depth)
    grouped = jnp.transpose(grouped, (1, 2, 0, 3)).reshape(query_rows, head_depth)
    message = jnp.concatenate((grouped, digits), axis=0)
    messages = [message] + [shifted(message, "seq", by) for by in range(1, seq_size)]

    weight_bytes = 2 * depth * 2 * kv_width
    flops = 4 * new_rows * depth * kv_width

    def project(rows, dtype):
        return call(
            functools.partial(project_body, len(rows)),
            sds((new_rows, 2 * kv_width), dtype),
            "project",
            flops,
            weight_bytes,
            0,
            len(rows) + 2,
        )(*rows, key_weight, value_weight)

    own_term = project([own_rows], f32)
    terms = []
    for by, half in enumerate(arrived):
        halves = [half] + [shifted(half, "head", head_size - turn) for turn in range(1, head_size)]
        terms.append(shifted(project(halves, bf16), "seq", seq_size - (by + 1)))

    score_scale = head_depth ** (-0.5)
    base = (seq_index * (cached_rows + new_rows)).astype(jnp.int32).reshape(1)
    every_row = seq_size * query_rows // local_kv
    stats = sds((local_kv, every_row, head_depth), f32)
    attend_flops = 4 * seq_size * query_rows * head_depth * cached_rows
    cached = call(
        functools.partial(cached_body, seq_size, text_rows, local_kv, score_scale),
        (stats, stats, stats),
        "cached",
        attend_flops,
        4 * cached_rows * kv_width,
        1,
        seq_size + 2,
        limit=40 << 20,
    )(
        base,
        *messages,
        key_cache.reshape(cached_rows, kv_width),
        value_cache.reshape(cached_rows, kv_width),
    )
    fresh = call(
        functools.partial(fresh_body, seq_size, text_rows, local_kv, head_size, score_scale),
        (sds((new_rows, kv_width), bf16),) * 2 + (sds((query_rows + 16, head_depth), bf16),) * seq_size,
        "fresh",
        attend_flops * new_rows // cached_rows,
        8 * every_row * kv_width,
        2,
        2 * seq_size + 4,
    )(
        base + cached_rows,
        head_index.astype(jnp.int32).reshape(1),
        *messages,
        own_term,
        *terms,
        key_gain.reshape(1, head_depth),
        *cached,
    )
    new_keys, new_values = (part.reshape(new_rows, local_kv, head_depth) for part in fresh[:2])
    returned = [fresh[2]] + [
        shifted(fresh[2 + by], "seq", seq_size - by) for by in range(1, seq_size)
    ]
    attended = call(
        functools.partial(merge_body, seq_size, text_rows),
        sds((text_rows, local_heads * head_depth), bf16),
        "merge",
        seq_size * query_rows * head_depth,
        2 * seq_size * query_rows * head_depth,
        0,
        seq_size,
    )(*returned)

    every = [attended] + [shifted(attended, "seq", by) for by in range(1, seq_size)]
    all_rows = seq_size * text_rows
    partial = call(
        functools.partial(output_body, seq_size),
        sds((all_rows, out_weight.shape[1]), f32),
        "output",
        2 * all_rows * out_weight.size,
        2 * out_weight.size,
        1,
        seq_size + 1,
        scratch=[pltpu.VMEM((all_rows, out_weight.shape[0]), f32)],
        limit=24 << 20,
    )(seq_index.astype(jnp.int32).reshape(1), *every, out_weight)

    out_rows = all_rows // (section_size * head_size)
    partial = partial.reshape(section_size, head_size, out_rows, -1)
    partial = summed_rows(jnp.swapaxes(partial, 0, 1), "head")
    layer_output = summed_rows(partial, "section").astype(bf16)
    return (layer_output, new_keys, new_values)


def solution(mesh):
    placed = (
        P(("groups", "seq"), ("section", "head"), None),
        P(("groups", "seq"), ("section", "head"), None),
        P(("groups", "seq"), ("section", "head"), None),
        P(("groups", "seq"), None),
        P("seq", ("section", "head")),
        P("seq", ("section", "head")),
        P(),
        P(("section", "head"), "seq"),
        P("groups"),
        P(("groups", "seq")),
    )
    return jax.shard_map(
        on_device,
        mesh=mesh,
        in_specs=placed,
        out_specs=(
            P(("groups", "section", "head"), "seq"),
            P(("groups", "seq"), ("section", "head"), None),
            P(("groups", "seq"), ("section", "head"), None),
        ),
        check_vma=False,
    )
```

```python
import functools

import jax
import jax.numpy as jnp
from jax import lax
from jax.experimental import pallas as pl
from jax.experimental.pallas import tpu as pltpu
from jax.sharding import PartitionSpec as P


masked_score = -1e30
norm_epsilon = 1e-05
bf16 = jnp.bfloat16
f32 = jnp.float32


def shifted(part, axis, by):
    peers = lax.axis_size(axis)
    return lax.ppermute(part, axis, [(i, (i + by) % peers) for i in range(peers)])


def block_at(array, index, axis=0):
    return lax.dynamic_index_in_dim(array, index, axis, keepdims=False)


def summed_rows(partial, axis):
    peers = lax.axis_size(axis)
    me = lax.axis_index(axis)
    total = block_at(partial, me)
    for by in range(1, peers):
        piece = block_at(partial, (me + by) % peers).astype(bf16)
        total = total + shifted(piece, axis, by).astype(f32)
    return total


vmem = pl.BlockSpec(memory_space=pltpu.VMEM)
hbm = pl.BlockSpec(memory_space=pltpu.HBM)


def call(body, outs, flops, moved, n_in, scratch=(), limit=None):
    return pl.pallas_call(
        body,
        out_shape=outs,
        in_specs=[vmem] * n_in,
        out_specs=jax.tree.map(lambda _: vmem, outs),
        scratch_shapes=list(scratch),
        cost_estimate=pl.CostEstimate(flops=flops, bytes_accessed=moved, transcendentals=0),
        compiler_params=pltpu.CompilerParams(vmem_limit_bytes=limit or (16 << 20)),
    )


def project_body(halves, blocks, *refs):
    row_refs, (key_ref, value_ref) = refs[:halves], refs[halves : halves + 2]
    extra_refs, out_ref = refs[halves + 2 : -1], refs[-1]
    rows = jnp.concatenate([ref[...] for ref in row_refs], axis=0)
    count = rows.shape[0]
    depth = out_ref.shape[1]
    kv = blocks // 2
    for i, ref in enumerate((key_ref, value_ref)):
        part = jnp.dot(rows, ref[...], preferred_element_type=f32).astype(out_ref.dtype)
        for c in range(kv):
            at = (i * kv + c) * count
            out_ref[at : at + count, :] = part[:, c * depth : (c + 1) * depth]
    for ref in extra_refs:
        out_ref[blocks * count :, :] = ref[...]


def prepare_body(pieces, *refs):
    feature_ref, query_ref, length_ref, frame_ref = refs[:4]
    piece_refs, message_ref = refs[4 : 4 + pieces], refs[4 + pieces]
    query_in, length_in, frame_in, query_wide, sems = refs[5 + pieces :]
    half_rows, depth = piece_refs[0].shape
    seq_size = pieces + 1
    rows = pl.ds(pl.multiple_of(lax.axis_index("head") * half_rows, half_rows), half_rows)
    copies = []
    for i, (source, target) in enumerate(
        ((query_ref, query_in), (length_ref, length_in), (frame_ref, frame_in))
    ):
        copies.append(pltpu.make_async_copy(source, target, sems.at[i]))
    for by, target in enumerate(piece_refs):
        at = lax.rem(lax.axis_index("seq") + (by + 1), seq_size)
        source = feature_ref.at[rows, pl.ds(pl.multiple_of(at * depth, depth), depth)]
        copies.append(pltpu.make_async_copy(source, target, sems.at[3 + by]))
    for copy in copies:
        copy.start()
    for copy in copies[:3]:
        copy.wait()
    text_rows = frame_in.shape[1]
    query_rows = query_in.shape[0]
    heads = query_rows // text_rows
    frames = length_in.shape[1]
    column = as_column(frame_in[...].astype(f32), diagonal(text_rows)).astype(jnp.int32)
    index = lax.broadcasted_iota(jnp.int32, (text_rows, frames), 1)
    seen = jnp.where(index <= column, length_in[...].astype(f32), 0.0)
    limit = jnp.sum(seen, axis=1, keepdims=True).astype(jnp.int32)
    lane = lax.broadcasted_iota(jnp.int32, (text_rows, query_in.shape[1]), 1)
    digits = jnp.where(lane == 0, limit & 255, 0)
    digits = jnp.where(lane == 1, (limit >> 8) & 255, digits)
    digits = jnp.where(lane == 2, limit >> 16, digits).astype(f32)
    blank = jnp.zeros((16 - text_rows, digits.shape[1]), f32)
    message_ref[query_rows:, :] = jnp.concatenate((digits, blank), axis=0).astype(bf16)
    query_wide[...] = query_in[...].astype(f32)
    for head in range(0, heads, 2):
        pair = [query_wide[pl.ds(head + i, text_rows, stride=heads), :] for i in range(2)]
        message_ref[head * text_rows : (head + 2) * text_rows, :] = jnp.concatenate(
            pair, axis=0
        ).astype(bf16)
    for copy in copies[3:]:
        copy.wait()


def own_body(blocks, *refs):
    feature_ref, *sources = refs[:4]
    *targets, term_ref, rows_ref, sems = refs[4:]
    depth = rows_ref.shape[1]
    columns = pl.ds(pl.multiple_of(lax.axis_index("seq") * depth, depth), depth)
    copies = [pltpu.make_async_copy(feature_ref.at[:, columns], rows_ref, sems.at[0])]
    for i in range(3):
        copies.append(pltpu.make_async_copy(sources[i], targets[i], sems.at[1 + i]))
    for copy in copies:
        copy.start()
    for copy in copies[:3]:
        copy.wait()
    project_body(1, blocks, rows_ref, targets[0], targets[1], term_ref)
    copies[3].wait()


def row_limits(message_refs, text_rows, query_rows, group):
    columns = []
    for ref in message_refs:
        digits = ref[query_rows:, :].astype(f32)[:text_rows]
        limit = digits[:, 0:1] + 256.0 * digits[:, 1:2] + 65536.0 * digits[:, 2:3]
        columns.extend([limit] * group)
    return jnp.concatenate(columns, axis=0).astype(jnp.int32)


def diagonal(size):
    shape = (size, size)
    return lax.broadcasted_iota(jnp.int32, shape, 0) == lax.broadcasted_iota(jnp.int32, shape, 1)


def store_logs(out_ref, start, query_rows, log):
    depth = out_ref.shape[1]
    if log.shape[1] < depth:
        log = jnp.concatenate((log, jnp.zeros((1, depth - log.shape[1]), f32)), axis=1)
    high = log.astype(bf16).astype(f32)
    middle = (log - high).astype(bf16).astype(f32)
    low = log - high - middle
    pieces = jnp.concatenate((high, middle, low, jnp.zeros((13, depth), f32)), axis=0)
    out_ref[start + query_rows :, :] = pieces.astype(bf16)


def read_logs(message, query_rows):
    pieces = message[query_rows:].astype(f32)
    return (pieces[0:1] + pieces[1:2] + pieces[2:3])[:, :query_rows]


def as_column(row, on_diagonal):
    return jnp.sum(jnp.where(on_diagonal, row, 0.0), axis=1, keepdims=True)


def cached_body(blocks, text_rows, kv, scale, block_keys, *refs):
    message_refs = refs[:blocks]
    key_ref, value_ref = refs[blocks : 2 + blocks]
    out_refs = refs[2 + blocks :]
    depth = message_refs[0].shape[1]
    query_rows = message_refs[0].shape[0] - 16
    unit = query_rows // kv
    group = unit // text_rows
    keys = key_ref.shape[0]
    step = min(blocks, 4)
    position = lax.broadcasted_iota(jnp.int32, (step * unit, keys), 1) + lax.axis_index("seq") * block_keys
    on_diagonal = diagonal(unit)
    for start in range(0, blocks, step):
        some = message_refs[start : start + step]
        visible = position < row_limits(some, text_rows, query_rows, group)
        logs = [[] for _ in some]
        for c in range(kv):
            query = jnp.concatenate([ref[c * unit : (c + 1) * unit, :] for ref in some], axis=0)
            lanes = slice(c * depth, (c + 1) * depth)
            scores = lax.dot_general(
                query, key_ref[:, lanes], (((1,), (1,)), ((), ())), preferred_element_type=f32
            ) * scale
            scores = jnp.where(visible, scores, masked_score)
            peak = jnp.max(scores, axis=1, keepdims=True)
            weights = jnp.where(visible, jnp.exp(scores - peak), 0.0)
            total = jnp.sum(weights, axis=1, keepdims=True)
            summed = jnp.dot(weights.astype(bf16), value_ref[:, lanes], preferred_element_type=f32)
            some_seen = total > 0.0
            safe = jnp.where(some_seen, total, 1.0)
            mean = (summed / safe).astype(bf16)
            log = jnp.where(some_seen, peak + jnp.log(safe), masked_score)
            for i in range(len(some)):
                rows = slice(i * unit, (i + 1) * unit)
                out_refs[start + i][c * unit : (c + 1) * unit, :] = mean[rows]
                logs[i].append(
                    jnp.sum(jnp.where(on_diagonal, log[rows], 0.0), axis=0, keepdims=True)
                )
        for i in range(len(some)):
            store_logs(out_refs[start + i], 0, query_rows, jnp.concatenate(logs[i], axis=1))


def owner_body(kv, halves, own_ref, gain_ref, mine_ref, *refs):
    term_refs, out_ref = refs[:-1], refs[-1]
    fresh_rows = own_ref.shape[0]
    count = fresh_rows // (2 * kv)
    query_rows = mine_ref.shape[0] - 16
    half = count // halves
    for c in range(2 * kv):
        at = slice(c * count, (c + 1) * count)
        raw = functools.reduce(jnp.add, [ref[at, :].astype(f32) for ref in term_refs])
        turned = raw
        for turn in range(1, halves):
            other = jnp.concatenate((raw[-turn * half :], raw[: -turn * half]), axis=0)
            turned = jnp.where(lax.axis_index("head") == turn, other, turned)
        raw = turned + own_ref[at, :]
        if c < kv:
            mean_square = jnp.mean(raw * raw, axis=1, keepdims=True)
            raw = raw * lax.rsqrt(mean_square + norm_epsilon) * gain_ref[...]
        out_ref[at, :] = raw.astype(bf16)
    messages = [mine_ref[...]] + [ref[fresh_rows:, :] for ref in term_refs]
    on_diagonal = diagonal(query_rows)
    logs = [read_logs(message, query_rows) for message in messages]
    top = functools.reduce(jnp.maximum, logs)
    shares = [jnp.exp(log - top) for log in logs]
    whole = functools.reduce(jnp.add, shares)
    merged = None
    for share, message in zip(shares, messages):
        term = as_column(share / whole, on_diagonal) * message[:query_rows].astype(f32)
        merged = term if merged is None else merged + term
    out_ref[fresh_rows : fresh_rows + query_rows, :] = merged.astype(bf16)
    store_logs(out_ref, fresh_rows, query_rows, top + jnp.log(whole))


def final_body(blocks, text_rows, kv, scale, block_keys, heads, sections, *refs):
    message_refs = refs[:blocks]
    fresh_refs = refs[blocks : 2 * blocks]
    weight_ref, sent_ref, kept_ref, rows_ref, product_ref = refs[2 * blocks :]
    depth = message_refs[0].shape[1]
    query_rows = message_refs[0].shape[0] - 16
    unit = query_rows // kv
    group = unit // text_rows
    fresh_rows = fresh_refs[0].shape[0] - query_rows - 16
    keys = fresh_rows // (2 * kv)
    me = lax.axis_index("seq")
    places = [lax.rem(me + (blocks - by), blocks) for by in range(blocks)]
    columns = lax.broadcasted_iota(jnp.int32, (1, keys), 1) + (block_keys - keys)
    position = jnp.concatenate([columns + place * block_keys for place in places], axis=1)
    on_diagonal = diagonal(query_rows)
    step = min(blocks, 4)
    for start in range(0, blocks, step):
        span = range(start, start + step)
        some = [message_refs[i] for i in span]
        visible = position < row_limits(some, text_rows, query_rows, group)
        logs = [
            as_column(read_logs(fresh_refs[i][fresh_rows:, :], query_rows), on_diagonal) for i in span
        ]
        for c in range(kv):
            part = slice(c * unit, (c + 1) * unit)
            key_part = slice(c * keys, (c + 1) * keys)
            value_part = slice((kv + c) * keys, (kv + c + 1) * keys)
            query = jnp.concatenate([ref[part, :] for ref in some], axis=0)
            key = jnp.concatenate([ref[key_part, :] for ref in fresh_refs], axis=0)
            value = jnp.concatenate([ref[value_part, :] for ref in fresh_refs], axis=0)
            scores = lax.dot_general(
                query, key, (((1,), (1,)), ((), ())), preferred_element_type=f32
            ) * scale
            scores = jnp.where(visible, scores, masked_score)
            old_log = jnp.concatenate([log[part] for log in logs], axis=0)
            peak = jnp.maximum(jnp.max(scores, axis=1, keepdims=True), old_log)
            weights = jnp.where(visible, jnp.exp(scores - peak), 0.0)
            share = jnp.exp(old_log - peak)
            total = share + jnp.sum(weights, axis=1, keepdims=True)
            old_part = slice(fresh_rows + c * unit, fresh_rows + (c + 1) * unit)
            old = jnp.concatenate([fresh_refs[i][old_part, :] for i in span], axis=0).astype(f32)
            summed = share * old + jnp.dot(
                weights.astype(bf16), value, preferred_element_type=f32
            )
            attended = summed / total
            for i in span:
                at = pl.ds(pl.multiple_of(places[i] * text_rows, text_rows), text_rows)
                for g in range(group):
                    row = (i - start) * unit + g * text_rows
                    col = (c * group + g) * depth
                    rows_ref[at, col : col + depth] = attended[row : row + text_rows]
    rows = rows_ref[...].astype(bf16)
    product_ref[...] = jnp.dot(rows, weight_ref[...], preferred_element_type=f32)
    count = product_ref.shape[0] // (heads * sections)
    mine = lax.axis_index("head")
    for s in range(sections):
        here = slice(s * count, (s + 1) * count)
        keep_at = pl.multiple_of((s * heads + mine) * count, count)
        kept_ref[here, :] = product_ref[pl.ds(keep_at, count), :]
        for by in range(1, heads):
            to = lax.rem(mine + by, heads)
            send_at = pl.multiple_of((s * heads + to) * count, count)
            there = slice(((by - 1) * sections + s) * count, ((by - 1) * sections + s + 1) * count)
            sent_ref[there, :] = product_ref[pl.ds(send_at, count), :].astype(bf16)


def on_device(
    queries,
    key_cache,
    value_cache,
    new_features,
    key_weight,
    value_weight,
    key_gain,
    out_weight,
    frame_length,
    text_frame,
):
    cached_rows, local_kv, head_depth = key_cache.shape
    kv_width = key_weight.shape[1]
    depth = key_weight.shape[0]
    new_rows = new_features.shape[0]
    text_rows, local_heads, _ = queries.shape
    query_rows = text_rows * local_heads
    seq_size = lax.axis_size("seq")
    head_size = lax.axis_size("head")
    section_size = lax.axis_size("section")
    half_rows = new_rows // head_size
    sds = jax.ShapeDtypeStruct

    pieces = seq_size - 1
    prepare = pl.pallas_call(
        functools.partial(prepare_body, pieces),
        out_shape=(sds((half_rows, depth), bf16),) * pieces
        + (sds((query_rows + 16, head_depth), bf16),),
        in_specs=[hbm] * 4,
        out_specs=(vmem,) * seq_size,
        scratch_shapes=[
            pltpu.VMEM((query_rows, head_depth), bf16),
            pltpu.VMEM((1, frame_length.shape[0]), jnp.int32),
            pltpu.VMEM((1, text_rows), jnp.int32),
            pltpu.VMEM((query_rows, head_depth), f32),
            pltpu.SemaphoreType.DMA((pieces + 3,)),
        ],
        name="prepare",
        cost_estimate=pl.CostEstimate(
            flops=0, bytes_accessed=8 * half_rows * depth, transcendentals=0
        ),
        compiler_params=pltpu.CompilerParams(vmem_limit_bytes=8 << 20),
    )
    sources = (
        new_features,
        queries.reshape(query_rows, head_depth),
        frame_length.reshape(1, -1),
        text_frame.reshape(1, -1),
    )
    *sent_pieces, message = prepare(
        *[pltpu.with_memory_space_constraint(w, pltpu.HBM) for w in sources],
    )
    arrived = [shifted(part, "seq", by + 1) for by, part in enumerate(sent_pieces)]
    messages = [message] + [shifted(message, "seq", by) for by in range(1, seq_size)]

    key_cache = key_cache.reshape(cached_rows, kv_width)
    value_cache = value_cache.reshape(cached_rows, kv_width)
    flops = 4 * new_rows * depth * kv_width

    kv_blocks = 2 * local_kv

    def project(rows, dtype, extra=()):
        extra_rows = sum(part.shape[0] for part in extra)
        return call(
            functools.partial(project_body, len(rows), kv_blocks),
            sds((kv_blocks * new_rows + extra_rows, head_depth), dtype),
            flops,
            4 * depth * kv_width,
            len(rows) + 2 + len(extra),
        )(*rows, key_weight, value_weight, *extra)

    sources = (new_features, key_weight, value_weight, out_weight)
    load = pl.pallas_call(
        functools.partial(own_body, kv_blocks),
        out_shape=(
            *(sds(w.shape, bf16) for w in sources[1:]),
            sds((kv_blocks * new_rows, head_depth), f32),
        ),
        in_specs=[hbm] * 4,
        out_specs=(vmem,) * 4,
        scratch_shapes=[pltpu.VMEM((new_rows, depth), bf16), pltpu.SemaphoreType.DMA((4,))],
        name="own",
        cost_estimate=pl.CostEstimate(
            flops=flops, bytes_accessed=4 * sum(w.size for w in sources[1:]), transcendentals=0
        ),
        compiler_params=pltpu.CompilerParams(vmem_limit_bytes=16 << 20),
    )
    sources = [pltpu.with_memory_space_constraint(w, pltpu.HBM) for w in sources]
    key_weight, value_weight, out_weight, own_term = load(*sources)

    score_scale = head_depth ** (-0.5)
    block_keys = cached_rows + new_rows
    attend_flops = 4 * seq_size * query_rows * head_depth * cached_rows
    message_shape = sds(message.shape, bf16)
    attend_cached = call(
        functools.partial(cached_body, seq_size, text_rows, local_kv, score_scale, block_keys),
        (message_shape,) * seq_size,
        attend_flops,
        4 * cached_rows * kv_width,
        seq_size + 2,
        limit=24 << 20,
    )
    cached = attend_cached(*messages, key_cache, value_cache)
    terms = []
    for by, half in enumerate(arrived):
        halves = [half] + [shifted(half, "head", head_size - turn) for turn in range(1, head_size)]
        term = project(halves, bf16, (cached[by + 1],))
        terms.append(shifted(term, "seq", seq_size - (by + 1)))
    fresh_rows = kv_blocks * new_rows
    fresh = call(
        functools.partial(owner_body, local_kv, head_size),
        sds((fresh_rows + query_rows + 16, head_depth), bf16),
        8 * new_rows * kv_width,
        4 * seq_size * new_rows * kv_width,
        seq_size + 2,
    )(
        own_term,
        key_gain.reshape(1, head_depth),
        cached[0],
        *terms,
    )
    fresh_all = [fresh] + [shifted(fresh, "seq", by) for by in range(1, seq_size)]
    made = fresh[:fresh_rows].reshape(2, local_kv, new_rows, head_depth)
    new_keys, new_values = (jnp.swapaxes(part, 0, 1) for part in made)

    all_rows = seq_size * text_rows
    out_width = out_weight.shape[1]
    out_rows = all_rows // (section_size * head_size)
    sent, kept = call(
        functools.partial(
            final_body,
            seq_size,
            text_rows,
            local_kv,
            score_scale,
            block_keys,
            head_size,
            section_size,
        ),
        (
            sds(((head_size - 1) * section_size * out_rows, out_width), bf16),
            sds((section_size * out_rows, out_width), f32),
        ),
        2 * all_rows * out_weight.size,
        2 * out_weight.size,
        2 * seq_size + 1,
        scratch=[
            pltpu.VMEM((all_rows, local_heads * head_depth), f32),
            pltpu.VMEM((all_rows, out_width), f32),
        ],
        limit=24 << 20,
    )(
        *messages,
        *fresh_all,
        out_weight,
    )
    sent = sent.reshape(head_size - 1, section_size * out_rows, out_width)
    for by in range(1, head_size):
        kept = kept + shifted(sent[by - 1], "head", by).astype(f32)
    layer_output = summed_rows(kept.reshape(section_size, out_rows, out_width), "section")
    return (layer_output.astype(bf16), new_keys, new_values)


def solution(mesh):
    placed = (
        P(("groups", "seq"), ("section", "head"), None),
        P(("groups", "seq"), ("section", "head"), None),
        P(("groups", "seq"), ("section", "head"), None),
        P(("groups", "seq"), None),
        P("seq", ("section", "head")),
        P("seq", ("section", "head")),
        P(),
        P(("section", "head"), "seq"),
        P("groups"),
        P(("groups", "seq")),
    )
    return jax.shard_map(
        on_device,
        mesh=mesh,
        in_specs=placed,
        out_specs=(
            P(("groups", "section", "head"), "seq"),
            P(("groups", "seq"), ("section", "head"), None),
            P(("groups", "seq"), ("section", "head"), None),
        ),
        check_vma=False,
    )
```

```python
import functools

import jax
import jax.numpy as jnp
from jax import lax
from jax.experimental import pallas as pl
from jax.experimental.pallas import tpu as pltpu
from jax.sharding import PartitionSpec as P


masked_score = -1e30
norm_epsilon = 1e-05
extra_rows = 8
bf16 = jnp.bfloat16
f32 = jnp.float32


def shifted(part, axis, by):
    peers = lax.axis_size(axis)
    return lax.ppermute(part, axis, [(i, (i + by) % peers) for i in range(peers)])


def swapped(part, by):
    peers = lax.axis_size("seq")
    return lax.ppermute(part, "seq", [(i, i ^ by) for i in range(peers)])


vmem = pl.BlockSpec(memory_space=pltpu.VMEM)
hbm = pl.BlockSpec(memory_space=pltpu.HBM)


def call(body, outs, flops, moved, n_in, scratch=(), limit=None):
    return pl.pallas_call(
        body,
        out_shape=outs,
        in_specs=[vmem] * n_in,
        out_specs=jax.tree.map(lambda _: vmem, outs),
        scratch_shapes=list(scratch),
        cost_estimate=pl.CostEstimate(flops=flops, bytes_accessed=moved, transcendentals=0),
        compiler_params=pltpu.CompilerParams(vmem_limit_bytes=limit or (16 << 20)),
    )


def project_body(pieces, halves, blocks, *refs):
    row_refs, (key_ref, value_ref) = refs[: pieces * halves], refs[pieces * halves :][:2]
    rest = refs[pieces * halves + 2 :]
    extra_refs, out_refs = rest[:-pieces], rest[-pieces:]
    rows = jnp.concatenate([ref[...] for ref in row_refs], axis=0)
    count = rows.shape[0] // pieces
    depth = out_refs[0].shape[1]
    kv = blocks // 2
    for i, ref in enumerate((key_ref, value_ref)):
        part = jnp.dot(rows, ref[...], preferred_element_type=f32).astype(out_refs[0].dtype)
        for c in range(kv):
            at = (i * kv + c) * count
            lanes = slice(c * depth, (c + 1) * depth)
            for piece, out_ref in enumerate(out_refs):
                out_ref[at : at + count, :] = part[piece * count : (piece + 1) * count, lanes]
    for ref, out_ref in zip(extra_refs, out_refs):
        out_ref[blocks * count :, :] = ref[...]


def prepare_body(pieces, *refs):
    feature_ref, query_ref, length_ref, frame_ref = refs[:4]
    piece_refs, message_ref = refs[4 : 4 + pieces], refs[4 + pieces]
    query_in, length_in, frame_in, query_wide, sems = refs[5 + pieces :]
    half_rows, depth = piece_refs[0].shape
    rows = pl.ds(pl.multiple_of(lax.axis_index("head") * half_rows, half_rows), half_rows)
    copies = []
    for i, (source, target) in enumerate(
        ((query_ref, query_in), (length_ref, length_in), (frame_ref, frame_in))
    ):
        copies.append(pltpu.make_async_copy(source, target, sems.at[i]))
    for by, target in enumerate(piece_refs):
        at = lax.axis_index("seq") ^ (by + 1)
        source = feature_ref.at[rows, pl.ds(pl.multiple_of(at * depth, depth), depth)]
        copies.append(pltpu.make_async_copy(source, target, sems.at[3 + by]))
    for copy in copies:
        copy.start()
    for copy in copies[:3]:
        copy.wait()
    text_rows = frame_in.shape[1]
    query_rows = query_in.shape[0]
    heads = query_rows // text_rows
    frames = length_in.shape[1]
    column = as_column(frame_in[...].astype(f32), diagonal(text_rows)).astype(jnp.int32)
    index = lax.broadcasted_iota(jnp.int32, (text_rows, frames), 1)
    seen = jnp.where(index <= column, length_in[...].astype(f32), 0.0)
    limit = jnp.sum(seen, axis=1, keepdims=True).astype(jnp.int32)
    lane = lax.broadcasted_iota(jnp.int32, (text_rows, query_in.shape[1]), 1)
    digits = jnp.where(lane == 0, limit & 255, 0)
    digits = jnp.where(lane == 1, (limit >> 8) & 255, digits)
    digits = jnp.where(lane == 2, limit >> 16, digits).astype(f32)
    message_ref[query_rows:, :] = digits.astype(bf16)
    query_wide[...] = query_in[...].astype(f32)
    for head in range(0, heads, 2):
        pair = [query_wide[pl.ds(head + i, text_rows, stride=heads), :] for i in range(2)]
        message_ref[head * text_rows : (head + 2) * text_rows, :] = jnp.concatenate(
            pair, axis=0
        ).astype(bf16)
    for copy in copies[3:]:
        copy.wait()


def own_body(blocks, *refs):
    feature_ref, *sources = refs[:4]
    *targets, term_ref, rows_ref, sems = refs[4:]
    depth = rows_ref.shape[1]
    columns = pl.ds(pl.multiple_of(lax.axis_index("seq") * depth, depth), depth)
    copies = [pltpu.make_async_copy(feature_ref.at[:, columns], rows_ref, sems.at[0])]
    for i in range(3):
        copies.append(pltpu.make_async_copy(sources[i], targets[i], sems.at[1 + i]))
    for copy in copies:
        copy.start()
    for copy in copies[:3]:
        copy.wait()
    project_body(1, 1, blocks, rows_ref, targets[0], targets[1], term_ref)
    copies[3].wait()


def row_limits(message_refs, text_rows, query_rows, group):
    columns = []
    for ref in message_refs:
        digits = ref[query_rows:, :].astype(f32)[:text_rows]
        limit = digits[:, 0:1] + 256.0 * digits[:, 1:2] + 65536.0 * digits[:, 2:3]
        columns.extend([limit] * group)
    return jnp.concatenate(columns, axis=0).astype(jnp.int32)


def diagonal(size):
    shape = (size, size)
    return lax.broadcasted_iota(jnp.int32, shape, 0) == lax.broadcasted_iota(jnp.int32, shape, 1)


def store_logs(out_ref, start, query_rows, log):
    depth = out_ref.shape[1]
    if log.shape[1] < depth:
        log = jnp.concatenate((log, jnp.zeros((1, depth - log.shape[1]), f32)), axis=1)
    high = log.astype(bf16).astype(f32)
    middle = (log - high).astype(bf16).astype(f32)
    low = log - high - middle
    pieces = jnp.concatenate((high, middle, low, jnp.zeros((extra_rows - 3, depth), f32)), axis=0)
    out_ref[start + query_rows :, :] = pieces.astype(bf16)


def read_logs(message, query_rows):
    pieces = message[query_rows:].astype(f32)
    return (pieces[0:1] + pieces[1:2] + pieces[2:3])[:, :query_rows]


def as_column(row, on_diagonal):
    return jnp.sum(jnp.where(on_diagonal, row, 0.0), axis=1, keepdims=True)


def cached_body(blocks, text_rows, kv, scale, block_keys, *refs):
    message_refs = refs[:blocks]
    key_ref, value_ref, mean_ref, log_ref = refs[blocks:]
    depth = message_refs[0].shape[1]
    query_rows = message_refs[0].shape[0] - extra_rows
    unit = query_rows // kv
    group = unit // text_rows
    keys = key_ref.shape[0]
    step = min(blocks, 4)
    base = lax.axis_index("seq") * block_keys
    position = lax.broadcasted_iota(jnp.int32, (step * unit, keys), 1) + base
    for start in range(0, blocks, step):
        some = message_refs[start : start + step]
        visible = position < row_limits(some, text_rows, query_rows, group)
        at = slice(start * unit, (start + step) * unit)
        for c in range(kv):
            query = jnp.concatenate([ref[c * unit : (c + 1) * unit, :] for ref in some], axis=0)
            lanes = slice(c * depth, (c + 1) * depth)
            scores = lax.dot_general(
                query, key_ref[:, lanes], (((1,), (1,)), ((), ())), preferred_element_type=f32
            ) * scale
            scores = jnp.where(visible, scores, masked_score)
            peak = jnp.max(scores, axis=1, keepdims=True)
            weights = jnp.where(visible, jnp.exp(scores - peak), 0.0)
            total = jnp.sum(weights, axis=1, keepdims=True)
            summed = jnp.dot(weights.astype(bf16), value_ref[:, lanes], preferred_element_type=f32)
            some_seen = total > 0.0
            safe = jnp.where(some_seen, total, 1.0)
            mean_ref[c, at, :] = summed / safe
            log = jnp.where(some_seen, peak + jnp.log(safe), masked_score)
            log_ref[c, at, :] = jnp.broadcast_to(log, summed.shape)


def fresh_body(blocks, text_rows, kv, halves, scale, block_keys, own_ref, gain_ref, *refs):
    term_refs, message_refs = refs[: blocks - 1], refs[blocks - 1 : 2 * blocks - 1]
    mean_ref, log_ref, fresh_ref, *out_refs = refs[2 * blocks - 1 :]
    keys = own_ref.shape[0] // (2 * kv)
    query_rows = message_refs[0].shape[0] - extra_rows
    unit = query_rows // kv
    group = unit // text_rows
    half = keys // halves
    parts = []
    for c in range(2 * kv):
        at = slice(c * keys, (c + 1) * keys)
        raw = functools.reduce(jnp.add, [ref[at, :].astype(f32) for ref in term_refs])
        turned = raw
        for turn in range(1, halves):
            other = jnp.concatenate((raw[-turn * half :], raw[: -turn * half]), axis=0)
            turned = jnp.where(lax.axis_index("head") == turn, other, turned)
        raw = turned + own_ref[at, :]
        if c < kv:
            mean_square = jnp.mean(raw * raw, axis=1, keepdims=True)
            raw = raw * lax.rsqrt(mean_square + norm_epsilon) * gain_ref[...]
        parts.append(raw.astype(bf16))
        fresh_ref[at, :] = parts[-1]
    step = min(blocks, 4)
    base = lax.axis_index("seq") * block_keys + (block_keys - keys)
    position = lax.broadcasted_iota(jnp.int32, (step * unit, keys), 1) + base
    on_diagonal = diagonal(unit)
    for start in range(0, blocks, step):
        some = message_refs[start : start + step]
        visible = position < row_limits(some, text_rows, query_rows, group)
        at = slice(start * unit, (start + step) * unit)
        logs = [[] for _ in some]
        for c in range(kv):
            query = jnp.concatenate([ref[c * unit : (c + 1) * unit, :] for ref in some], axis=0)
            scores = lax.dot_general(
                query, parts[c], (((1,), (1,)), ((), ())), preferred_element_type=f32
            ) * scale
            scores = jnp.where(visible, scores, masked_score)
            old_log = log_ref[c, at, :1]
            peak = jnp.maximum(jnp.max(scores, axis=1, keepdims=True), old_log)
            weights = jnp.where(visible, jnp.exp(scores - peak), 0.0)
            share = jnp.exp(old_log - peak)
            total = share + jnp.sum(weights, axis=1, keepdims=True)
            summed = share * mean_ref[c, at, :] + jnp.dot(
                weights.astype(bf16), parts[kv + c], preferred_element_type=f32
            )
            mean = (summed / total).astype(bf16)
            log = peak + jnp.log(total)
            for i in range(len(some)):
                rows = slice(i * unit, (i + 1) * unit)
                out_refs[start + i][c * unit : (c + 1) * unit, :] = mean[rows]
                logs[i].append(
                    jnp.sum(jnp.where(on_diagonal, log[rows], 0.0), axis=0, keepdims=True)
                )
        for i in range(len(some)):
            store_logs(out_refs[start + i], 0, query_rows, jnp.concatenate(logs[i], axis=1))


def merge_body(blocks, text_rows, *refs):
    message_refs, out_ref = refs[:blocks], refs[blocks]
    depth = message_refs[0].shape[1]
    query_rows = message_refs[0].shape[0] - extra_rows
    on_diagonal = diagonal(query_rows)
    logs = [read_logs(ref[...], query_rows) for ref in message_refs]
    top = functools.reduce(jnp.maximum, logs)
    shares = [jnp.exp(log - top) for log in logs]
    whole = functools.reduce(jnp.add, shares)
    merged = None
    for share, ref in zip(shares, message_refs):
        term = as_column(share / whole, on_diagonal) * ref[:query_rows, :].astype(f32)
        merged = term if merged is None else merged + term
    for head in range(query_rows // text_rows):
        lanes = slice(head * depth, (head + 1) * depth)
        out_ref[:, lanes] = merged[head * text_rows : (head + 1) * text_rows].astype(bf16)


def output_body(blocks, heads, sections, *refs):
    row_refs = refs[:blocks]
    weight_ref, sent_ref, kept_ref, rows_ref, product_ref = refs[blocks:]
    count = row_refs[0].shape[0]
    for by, ref in enumerate(row_refs):
        place = lax.axis_index("seq") ^ by
        at = pl.ds(pl.multiple_of(place * count, count), count)
        rows_ref[at, :] = ref[...].astype(f32)
    rows = rows_ref[...].astype(bf16)
    product_ref[...] = jnp.dot(rows, weight_ref[...], preferred_element_type=f32)
    count = product_ref.shape[0] // (heads * sections)
    mine = lax.axis_index("head")
    for s in range(sections):
        here = slice(s * count, (s + 1) * count)
        keep_at = pl.multiple_of((s * heads + mine) * count, count)
        kept_ref[here, :] = product_ref[pl.ds(keep_at, count), :]
        for by in range(1, heads):
            to = lax.rem(mine + by, heads)
            send_at = pl.multiple_of((s * heads + to) * count, count)
            there = slice(((by - 1) * sections + s) * count, ((by - 1) * sections + s + 1) * count)
            sent_ref[there, :] = product_ref[pl.ds(send_at, count), :].astype(bf16)


def turn_body(sections, kept_ref, *refs):
    got_refs, (sent_ref, own_ref, whole_ref) = refs[:-3], refs[-3:]
    total = kept_ref[...]
    for ref in got_refs:
        total = total + ref[...].astype(f32)
    whole_ref[...] = total
    count = own_ref.shape[0]
    me = lax.axis_index("section")
    own_ref[...] = whole_ref[pl.ds(pl.multiple_of(me * count, count), count), :]
    for by in range(1, sections):
        to = lax.rem(me + by, sections)
        there = slice((by - 1) * count, by * count)
        sent_ref[there, :] = whole_ref[pl.ds(pl.multiple_of(to * count, count), count), :].astype(bf16)


def on_device(
    queries,
    key_cache,
    value_cache,
    new_features,
    key_weight,
    value_weight,
    key_gain,
    out_weight,
    frame_length,
    text_frame,
):
    cached_rows, local_kv, head_depth = key_cache.shape
    kv_width = key_weight.shape[1]
    depth = key_weight.shape[0]
    new_rows = new_features.shape[0]
    text_rows, local_heads, _ = queries.shape
    query_rows = text_rows * local_heads
    seq_size = lax.axis_size("seq")
    head_size = lax.axis_size("head")
    section_size = lax.axis_size("section")
    half_rows = new_rows // head_size
    if seq_size & (seq_size - 1):
        raise ValueError("seq size")
    sds = jax.ShapeDtypeStruct

    pieces = seq_size - 1
    prepare = pl.pallas_call(
        functools.partial(prepare_body, pieces),
        out_shape=(sds((half_rows, depth), bf16),) * pieces
        + (sds((query_rows + extra_rows, head_depth), bf16),),
        in_specs=[hbm] * 4,
        out_specs=(vmem,) * seq_size,
        scratch_shapes=[
            pltpu.VMEM((query_rows, head_depth), bf16),
            pltpu.VMEM((1, frame_length.shape[0]), jnp.int32),
            pltpu.VMEM((1, text_rows), jnp.int32),
            pltpu.VMEM((query_rows, head_depth), f32),
            pltpu.SemaphoreType.DMA((pieces + 3,)),
        ],
        name="prepare",
        cost_estimate=pl.CostEstimate(
            flops=0, bytes_accessed=8 * half_rows * depth, transcendentals=0
        ),
        compiler_params=pltpu.CompilerParams(vmem_limit_bytes=8 << 20),
    )
    sources = (
        new_features,
        queries.reshape(query_rows, head_depth),
        frame_length.reshape(1, -1),
        text_frame.reshape(1, -1),
    )
    *sent_pieces, message = prepare(
        *[pltpu.with_memory_space_constraint(w, pltpu.HBM) for w in sources],
    )
    arrived = [swapped(part, by + 1) for by, part in enumerate(sent_pieces)]
    messages = [message] + [swapped(message, by) for by in range(1, seq_size)]

    key_cache = key_cache.reshape(cached_rows, kv_width)
    value_cache = value_cache.reshape(cached_rows, kv_width)
    flops = 4 * new_rows * depth * kv_width

    kv_blocks = 2 * local_kv

    sources = (new_features, key_weight, value_weight, out_weight)
    load = pl.pallas_call(
        functools.partial(own_body, kv_blocks),
        out_shape=(
            *(sds(w.shape, bf16) for w in sources[1:]),
            sds((kv_blocks * new_rows, head_depth), f32),
        ),
        in_specs=[hbm] * 4,
        out_specs=(vmem,) * 4,
        scratch_shapes=[pltpu.VMEM((new_rows, depth), bf16), pltpu.SemaphoreType.DMA((4,))],
        name="own",
        cost_estimate=pl.CostEstimate(
            flops=flops, bytes_accessed=4 * sum(w.size for w in sources[1:]), transcendentals=0
        ),
        compiler_params=pltpu.CompilerParams(vmem_limit_bytes=16 << 20),
    )
    sources = [pltpu.with_memory_space_constraint(w, pltpu.HBM) for w in sources]
    key_weight, value_weight, out_weight, own_term = load(*sources)

    score_scale = head_depth ** (-0.5)
    block_keys = cached_rows + new_rows
    attend_flops = 4 * seq_size * query_rows * head_depth * cached_rows
    every_row = seq_size * query_rows // local_kv
    state = sds((local_kv, every_row, head_depth), f32)
    attend_cached = call(
        functools.partial(cached_body, seq_size, text_rows, local_kv, score_scale, block_keys),
        (state, state),
        attend_flops,
        4 * cached_rows * kv_width,
        seq_size + 2,
        limit=24 << 20,
    )
    cached = attend_cached(*messages, key_cache, value_cache)
    rows = []
    for half in arrived:
        rows.append(half)
        for turn in range(1, head_size):
            rows.append(shifted(half, "head", head_size - turn))
    term_shape = sds((kv_blocks * new_rows, head_depth), bf16)
    terms = call(
        functools.partial(project_body, pieces, head_size, kv_blocks),
        (term_shape,) * pieces,
        flops * pieces,
        4 * depth * kv_width,
        pieces * head_size + 2,
    )(*rows, key_weight, value_weight)
    terms = [swapped(term, by + 1) for by, term in enumerate(terms)]
    fresh, *outgoing = call(
        functools.partial(
            fresh_body, seq_size, text_rows, local_kv, head_size, score_scale, block_keys
        ),
        (sds((kv_blocks * new_rows, head_depth), bf16),)
        + (sds(message.shape, bf16),) * seq_size,
        attend_flops * new_rows // cached_rows,
        8 * every_row * kv_width,
        2 * seq_size + 3,
    )(own_term, key_gain.reshape(1, head_depth), *terms, *messages, *cached)
    made = fresh.reshape(2, local_kv, new_rows, head_depth)
    new_keys, new_values = (jnp.swapaxes(part, 0, 1) for part in made)
    crossed = [outgoing[0]] + [swapped(outgoing[by], by) for by in range(1, seq_size)]
    attended = call(
        functools.partial(merge_body, seq_size, text_rows),
        sds((text_rows, local_heads * head_depth), bf16),
        seq_size * query_rows * head_depth,
        2 * seq_size * query_rows * head_depth,
        seq_size,
    )(*crossed)
    every = [attended] + [swapped(attended, by) for by in range(1, seq_size)]

    all_rows = seq_size * text_rows
    out_width = out_weight.shape[1]
    out_rows = all_rows // (section_size * head_size)
    sent, kept = call(
        functools.partial(output_body, seq_size, head_size, section_size),
        (
            sds(((head_size - 1) * section_size * out_rows, out_width), bf16),
            sds((section_size * out_rows, out_width), f32),
        ),
        2 * all_rows * out_weight.size,
        2 * out_weight.size,
        seq_size + 1,
        scratch=[
            pltpu.VMEM((all_rows, local_heads * head_depth), f32),
            pltpu.VMEM((all_rows, out_width), f32),
        ],
        limit=24 << 20,
    )(
        *every,
        out_weight,
    )
    sent = sent.reshape(head_size - 1, section_size * out_rows, out_width)
    got = [shifted(sent[by - 1], "head", by) for by in range(1, head_size)]
    sent, own_rows = call(
        functools.partial(turn_body, section_size),
        (
            sds(((section_size - 1) * out_rows, out_width), bf16),
            sds((out_rows, out_width), f32),
        ),
        kept.size,
        8 * kept.size,
        head_size,
        scratch=[pltpu.VMEM(kept.shape, f32)],
    )(kept, *got)
    sent = sent.reshape(section_size - 1, out_rows, out_width)
    for by in range(1, section_size):
        own_rows = own_rows + shifted(sent[by - 1], "section", by).astype(f32)
    return (own_rows.astype(bf16), new_keys, new_values)


def solution(mesh):
    placed = (
        P(("groups", "seq"), ("section", "head"), None),
        P(("groups", "seq"), ("section", "head"), None),
        P(("groups", "seq"), ("section", "head"), None),
        P(("groups", "seq"), None),
        P("seq", ("section", "head")),
        P("seq", ("section", "head")),
        P(),
        P(("section", "head"), "seq"),
        P("groups"),
        P(("groups", "seq")),
    )
    return jax.shard_map(
        on_device,
        mesh=mesh,
        in_specs=placed,
        out_specs=(
            P(("groups", "section", "head"), "seq"),
            P(("groups", "seq"), ("section", "head"), None),
            P(("groups", "seq"), ("section", "head"), None),
        ),
        check_vma=False,
    )
```

```python
import functools

import jax
import jax.numpy as jnp
from jax import lax
from jax.experimental import pallas as pl
from jax.experimental.pallas import tpu as pltpu
from jax.sharding import PartitionSpec as P


masked_score = -1e30
norm_epsilon = 1e-05
extra_rows = 8
bf16 = jnp.bfloat16
f32 = jnp.float32


def shifted(part, axis, by):
    peers = lax.axis_size(axis)
    return lax.ppermute(part, axis, [(i, (i + by) % peers) for i in range(peers)])


def swapped(part, by):
    peers = lax.axis_size("seq")
    return lax.ppermute(part, "seq", [(i, i ^ by) for i in range(peers)])


vmem = pl.BlockSpec(memory_space=pltpu.VMEM)
hbm = pl.BlockSpec(memory_space=pltpu.HBM)


def call(body, outs, flops, moved, n_in, scratch=(), limit=None):
    return pl.pallas_call(
        body,
        out_shape=outs,
        in_specs=[vmem] * n_in,
        out_specs=jax.tree.map(lambda _: vmem, outs),
        scratch_shapes=list(scratch),
        cost_estimate=pl.CostEstimate(flops=flops, bytes_accessed=moved, transcendentals=0),
        compiler_params=pltpu.CompilerParams(vmem_limit_bytes=limit or (16 << 20)),
    )


def project_body(pieces, halves, blocks, *refs):
    row_refs, (key_ref, value_ref) = refs[: pieces * halves], refs[pieces * halves :][:2]
    rest = refs[pieces * halves + 2 :]
    extra_refs, out_refs = rest[:-pieces], rest[-pieces:]
    rows = jnp.concatenate([ref[...] for ref in row_refs], axis=0)
    count = rows.shape[0] // pieces
    depth = out_refs[0].shape[1]
    kv = blocks // 2
    for i, ref in enumerate((key_ref, value_ref)):
        part = jnp.dot(rows, ref[...], preferred_element_type=f32).astype(out_refs[0].dtype)
        for c in range(kv):
            at = (i * kv + c) * count
            lanes = slice(c * depth, (c + 1) * depth)
            for piece, out_ref in enumerate(out_refs):
                out_ref[at : at + count, :] = part[piece * count : (piece + 1) * count, lanes]
    for ref, out_ref in zip(extra_refs, out_refs):
        out_ref[blocks * count :, :] = ref[...]


def cut_body(pieces, feature_ref, *refs):
    piece_refs, sems = refs[:pieces], refs[pieces]
    half_rows, depth = piece_refs[0].shape
    rows = pl.ds(pl.multiple_of(lax.axis_index("head") * half_rows, half_rows), half_rows)
    copies = []
    for by, target in enumerate(piece_refs):
        at = lax.axis_index("seq") ^ (by + 1)
        source = feature_ref.at[rows, pl.ds(pl.multiple_of(at * depth, depth), depth)]
        copies.append(pltpu.make_async_copy(source, target, sems.at[by]))
    for copy in copies:
        copy.start()
    for copy in copies:
        copy.wait()


def ask_body(query_ref, length_ref, frame_ref, message_ref, *scratch):
    query_in, length_in, frame_in, query_wide, sems = scratch
    copies = []
    for i, (source, target) in enumerate(
        ((query_ref, query_in), (length_ref, length_in), (frame_ref, frame_in))
    ):
        copies.append(pltpu.make_async_copy(source, target, sems.at[i]))
    for copy in copies:
        copy.start()
    for copy in copies:
        copy.wait()
    text_rows = frame_in.shape[1]
    query_rows = query_in.shape[0]
    heads = query_rows // text_rows
    frames = length_in.shape[1]
    column = as_column(frame_in[...].astype(f32), diagonal(text_rows)).astype(jnp.int32)
    index = lax.broadcasted_iota(jnp.int32, (text_rows, frames), 1)
    seen = jnp.where(index <= column, length_in[...].astype(f32), 0.0)
    limit = jnp.sum(seen, axis=1, keepdims=True).astype(jnp.int32)
    lane = lax.broadcasted_iota(jnp.int32, (text_rows, query_in.shape[1]), 1)
    digits = jnp.where(lane == 0, limit & 255, 0)
    digits = jnp.where(lane == 1, (limit >> 8) & 255, digits)
    digits = jnp.where(lane == 2, limit >> 16, digits).astype(f32)
    message_ref[query_rows:, :] = digits.astype(bf16)
    query_wide[...] = query_in[...].astype(f32)
    for head in range(0, heads, 2):
        pair = [query_wide[pl.ds(head + i, text_rows, stride=heads), :] for i in range(2)]
        message_ref[head * text_rows : (head + 2) * text_rows, :] = jnp.concatenate(
            pair, axis=0
        ).astype(bf16)


def own_body(blocks, *refs):
    feature_ref, *sources = refs[:4]
    *targets, term_ref, rows_ref, sems = refs[4:]
    depth = rows_ref.shape[1]
    columns = pl.ds(pl.multiple_of(lax.axis_index("seq") * depth, depth), depth)
    copies = [pltpu.make_async_copy(feature_ref.at[:, columns], rows_ref, sems.at[0])]
    for i in range(3):
        copies.append(pltpu.make_async_copy(sources[i], targets[i], sems.at[1 + i]))
    for copy in copies:
        copy.start()
    for copy in copies[:3]:
        copy.wait()
    project_body(1, 1, blocks, rows_ref, targets[0], targets[1], term_ref)
    copies[3].wait()


def row_limits(message_refs, text_rows, query_rows, group):
    columns = []
    for ref in message_refs:
        digits = ref[query_rows:, :].astype(f32)[:text_rows]
        limit = digits[:, 0:1] + 256.0 * digits[:, 1:2] + 65536.0 * digits[:, 2:3]
        columns.extend([limit] * group)
    return jnp.concatenate(columns, axis=0).astype(jnp.int32)


def diagonal(size):
    shape = (size, size)
    return lax.broadcasted_iota(jnp.int32, shape, 0) == lax.broadcasted_iota(jnp.int32, shape, 1)


def store_logs(out_ref, start, query_rows, log):
    depth = out_ref.shape[1]
    if log.shape[1] < depth:
        log = jnp.concatenate((log, jnp.zeros((1, depth - log.shape[1]), f32)), axis=1)
    high = log.astype(bf16).astype(f32)
    middle = (log - high).astype(bf16).astype(f32)
    low = log - high - middle
    pieces = jnp.concatenate((high, middle, low, jnp.zeros((extra_rows - 3, depth), f32)), axis=0)
    out_ref[start + query_rows :, :] = pieces.astype(bf16)


def read_logs(message, query_rows):
    pieces = message[query_rows:].astype(f32)
    return (pieces[0:1] + pieces[1:2] + pieces[2:3])[:, :query_rows]


def as_column(row, on_diagonal):
    return jnp.sum(jnp.where(on_diagonal, row, 0.0), axis=1, keepdims=True)


def cached_body(blocks, text_rows, kv, scale, block_keys, *refs):
    message_refs = refs[:blocks]
    key_ref, value_ref, mean_ref, log_ref = refs[blocks:]
    depth = message_refs[0].shape[1]
    query_rows = message_refs[0].shape[0] - extra_rows
    unit = query_rows // kv
    group = unit // text_rows
    keys = key_ref.shape[0]
    step = min(blocks, 4)
    base = lax.axis_index("seq") * block_keys
    position = lax.broadcasted_iota(jnp.int32, (step * unit, keys), 1) + base
    for start in range(0, blocks, step):
        some = message_refs[start : start + step]
        visible = position < row_limits(some, text_rows, query_rows, group)
        at = slice(start * unit, (start + step) * unit)
        for c in range(kv):
            query = jnp.concatenate([ref[c * unit : (c + 1) * unit, :] for ref in some], axis=0)
            lanes = slice(c * depth, (c + 1) * depth)
            scores = lax.dot_general(
                query, key_ref[:, lanes], (((1,), (1,)), ((), ())), preferred_element_type=f32
            ) * scale
            scores = jnp.where(visible, scores, masked_score)
            peak = jnp.max(scores, axis=1, keepdims=True)
            weights = jnp.where(visible, jnp.exp(scores - peak), 0.0)
            total = jnp.sum(weights, axis=1, keepdims=True)
            summed = jnp.dot(weights.astype(bf16), value_ref[:, lanes], preferred_element_type=f32)
            some_seen = total > 0.0
            safe = jnp.where(some_seen, total, 1.0)
            mean_ref[c, at, :] = summed / safe
            log = jnp.where(some_seen, peak + jnp.log(safe), masked_score)
            log_ref[c, at, :] = jnp.broadcast_to(log, summed.shape)


def fresh_body(blocks, text_rows, kv, halves, scale, block_keys, own_ref, gain_ref, *refs):
    term_refs, message_refs = refs[: blocks - 1], refs[blocks - 1 : 2 * blocks - 1]
    mean_ref, log_ref, fresh_ref, *out_refs = refs[2 * blocks - 1 :]
    keys = own_ref.shape[0] // (2 * kv)
    query_rows = message_refs[0].shape[0] - extra_rows
    unit = query_rows // kv
    group = unit // text_rows
    half = keys // halves
    parts = []
    for c in range(2 * kv):
        at = slice(c * keys, (c + 1) * keys)
        raw = functools.reduce(jnp.add, [ref[at, :].astype(f32) for ref in term_refs])
        turned = raw
        for turn in range(1, halves):
            other = jnp.concatenate((raw[-turn * half :], raw[: -turn * half]), axis=0)
            turned = jnp.where(lax.axis_index("head") == turn, other, turned)
        raw = turned + own_ref[at, :]
        if c < kv:
            mean_square = jnp.mean(raw * raw, axis=1, keepdims=True)
            raw = raw * lax.rsqrt(mean_square + norm_epsilon) * gain_ref[...]
        parts.append(raw.astype(bf16))
        fresh_ref[at, :] = parts[-1]
    step = min(blocks, 4)
    base = lax.axis_index("seq") * block_keys + (block_keys - keys)
    position = lax.broadcasted_iota(jnp.int32, (step * unit, keys), 1) + base
    on_diagonal = diagonal(unit)
    for start in range(0, blocks, step):
        some = message_refs[start : start + step]
        visible = position < row_limits(some, text_rows, query_rows, group)
        at = slice(start * unit, (start + step) * unit)
        logs = [[] for _ in some]
        for c in range(kv):
            query = jnp.concatenate([ref[c * unit : (c + 1) * unit, :] for ref in some], axis=0)
            scores = lax.dot_general(
                query, parts[c], (((1,), (1,)), ((), ())), preferred_element_type=f32
            ) * scale
            scores = jnp.where(visible, scores, masked_score)
            old_log = log_ref[c, at, :1]
            peak = jnp.maximum(jnp.max(scores, axis=1, keepdims=True), old_log)
            weights = jnp.where(visible, jnp.exp(scores - peak), 0.0)
            share = jnp.exp(old_log - peak)
            total = share + jnp.sum(weights, axis=1, keepdims=True)
            summed = share * mean_ref[c, at, :] + jnp.dot(
                weights.astype(bf16), parts[kv + c], preferred_element_type=f32
            )
            mean = (summed / total).astype(bf16)
            log = peak + jnp.log(total)
            for i in range(len(some)):
                rows = slice(i * unit, (i + 1) * unit)
                out_refs[start + i][c * unit : (c + 1) * unit, :] = mean[rows]
                logs[i].append(
                    jnp.sum(jnp.where(on_diagonal, log[rows], 0.0), axis=0, keepdims=True)
                )
        for i in range(len(some)):
            store_logs(out_refs[start + i], 0, query_rows, jnp.concatenate(logs[i], axis=1))


def merge_body(blocks, text_rows, *refs):
    message_refs, out_ref = refs[:blocks], refs[blocks]
    depth = message_refs[0].shape[1]
    query_rows = message_refs[0].shape[0] - extra_rows
    on_diagonal = diagonal(query_rows)
    logs = [read_logs(ref[...], query_rows) for ref in message_refs]
    top = functools.reduce(jnp.maximum, logs)
    shares = [jnp.exp(log - top) for log in logs]
    whole = functools.reduce(jnp.add, shares)
    merged = None
    for share, ref in zip(shares, message_refs):
        term = as_column(share / whole, on_diagonal) * ref[:query_rows, :].astype(f32)
        merged = term if merged is None else merged + term
    for head in range(query_rows // text_rows):
        lanes = slice(head * depth, (head + 1) * depth)
        out_ref[:, lanes] = merged[head * text_rows : (head + 1) * text_rows].astype(bf16)


def output_body(blocks, heads, sections, *refs):
    row_refs = refs[:blocks]
    weight_ref, sent_ref, kept_ref, rows_ref, product_ref = refs[blocks:]
    count = row_refs[0].shape[0]
    for by, ref in enumerate(row_refs):
        place = lax.axis_index("seq") ^ by
        at = pl.ds(pl.multiple_of(place * count, count), count)
        rows_ref[at, :] = ref[...].astype(f32)
    rows = rows_ref[...].astype(bf16)
    product_ref[...] = jnp.dot(rows, weight_ref[...], preferred_element_type=f32)
    count = product_ref.shape[0] // (heads * sections)
    mine = lax.axis_index("head")
    for s in range(sections):
        here = slice(s * count, (s + 1) * count)
        keep_at = pl.multiple_of((s * heads + mine) * count, count)
        kept_ref[here, :] = product_ref[pl.ds(keep_at, count), :]
        for by in range(1, heads):
            to = lax.rem(mine + by, heads)
            send_at = pl.multiple_of((s * heads + to) * count, count)
            there = slice(((by - 1) * sections + s) * count, ((by - 1) * sections + s + 1) * count)
            sent_ref[there, :] = product_ref[pl.ds(send_at, count), :].astype(bf16)


def turn_body(sections, kept_ref, *refs):
    got_refs, (sent_ref, own_ref, whole_ref) = refs[:-3], refs[-3:]
    total = kept_ref[...]
    for ref in got_refs:
        total = total + ref[...].astype(f32)
    whole_ref[...] = total
    count = own_ref.shape[0]
    me = lax.axis_index("section")
    own_ref[...] = whole_ref[pl.ds(pl.multiple_of(me * count, count), count), :]
    for by in range(1, sections):
        to = lax.rem(me + by, sections)
        there = slice((by - 1) * count, by * count)
        sent_ref[there, :] = whole_ref[pl.ds(pl.multiple_of(to * count, count), count), :].astype(bf16)


def on_device(
    queries,
    key_cache,
    value_cache,
    new_features,
    key_weight,
    value_weight,
    key_gain,
    out_weight,
    frame_length,
    text_frame,
):
    cached_rows, local_kv, head_depth = key_cache.shape
    kv_width = key_weight.shape[1]
    depth = key_weight.shape[0]
    new_rows = new_features.shape[0]
    text_rows, local_heads, _ = queries.shape
    query_rows = text_rows * local_heads
    seq_size = lax.axis_size("seq")
    head_size = lax.axis_size("head")
    section_size = lax.axis_size("section")
    half_rows = new_rows // head_size
    if seq_size & (seq_size - 1):
        raise ValueError("seq size")
    sds = jax.ShapeDtypeStruct

    pieces = seq_size - 1
    cut = pl.pallas_call(
        functools.partial(cut_body, pieces),
        out_shape=(sds((half_rows, depth), bf16),) * pieces,
        in_specs=[hbm],
        out_specs=(vmem,) * pieces,
        scratch_shapes=[pltpu.SemaphoreType.DMA((pieces,))],
        name="prepare",
        cost_estimate=pl.CostEstimate(
            flops=0, bytes_accessed=8 * half_rows * depth, transcendentals=0
        ),
        compiler_params=pltpu.CompilerParams(vmem_limit_bytes=8 << 20),
    )
    sent_pieces = cut(pltpu.with_memory_space_constraint(new_features, pltpu.HBM))
    ask = pl.pallas_call(
        ask_body,
        out_shape=sds((query_rows + extra_rows, head_depth), bf16),
        in_specs=[hbm] * 3,
        out_specs=vmem,
        scratch_shapes=[
            pltpu.VMEM((query_rows, head_depth), bf16),
            pltpu.VMEM((1, frame_length.shape[0]), jnp.int32),
            pltpu.VMEM((1, text_rows), jnp.int32),
            pltpu.VMEM((query_rows, head_depth), f32),
            pltpu.SemaphoreType.DMA((3,)),
        ],
        name="ask",
        cost_estimate=pl.CostEstimate(
            flops=0, bytes_accessed=8 * query_rows * head_depth, transcendentals=0
        ),
        compiler_params=pltpu.CompilerParams(vmem_limit_bytes=8 << 20),
    )
    sources = (
        queries.reshape(query_rows, head_depth),
        frame_length.reshape(1, -1),
        text_frame.reshape(1, -1),
    )
    message = ask(*[pltpu.with_memory_space_constraint(w, pltpu.HBM) for w in sources])
    arrived = [swapped(part, by + 1) for by, part in enumerate(sent_pieces)]
    messages = [message] + [swapped(message, by) for by in range(1, seq_size)]

    key_cache = key_cache.reshape(cached_rows, kv_width)
    value_cache = value_cache.reshape(cached_rows, kv_width)
    flops = 4 * new_rows * depth * kv_width

    kv_blocks = 2 * local_kv

    sources = (new_features, key_weight, value_weight, out_weight)
    load = pl.pallas_call(
        functools.partial(own_body, kv_blocks),
        out_shape=(
            *(sds(w.shape, bf16) for w in sources[1:]),
            sds((kv_blocks * new_rows, head_depth), f32),
        ),
        in_specs=[hbm] * 4,
        out_specs=(vmem,) * 4,
        scratch_shapes=[pltpu.VMEM((new_rows, depth), bf16), pltpu.SemaphoreType.DMA((4,))],
        name="own",
        cost_estimate=pl.CostEstimate(
            flops=flops, bytes_accessed=4 * sum(w.size for w in sources[1:]), transcendentals=0
        ),
        compiler_params=pltpu.CompilerParams(vmem_limit_bytes=16 << 20),
    )
    sources = [pltpu.with_memory_space_constraint(w, pltpu.HBM) for w in sources]
    key_weight, value_weight, out_weight, own_term = load(*sources)

    score_scale = head_depth ** (-0.5)
    block_keys = cached_rows + new_rows
    attend_flops = 4 * seq_size * query_rows * head_depth * cached_rows
    every_row = seq_size * query_rows // local_kv
    state = sds((local_kv, every_row, head_depth), f32)
    attend_cached = call(
        functools.partial(cached_body, seq_size, text_rows, local_kv, score_scale, block_keys),
        (state, state),
        attend_flops,
        4 * cached_rows * kv_width,
        seq_size + 2,
        limit=24 << 20,
    )
    cached = attend_cached(*messages, key_cache, value_cache)
    rows = []
    for half in arrived:
        rows.append(half)
        for turn in range(1, head_size):
            rows.append(shifted(half, "head", head_size - turn))
    term_shape = sds((kv_blocks * new_rows, head_depth), bf16)
    terms = call(
        functools.partial(project_body, pieces, head_size, kv_blocks),
        (term_shape,) * pieces,
        flops * pieces,
        4 * depth * kv_width,
        pieces * head_size + 2,
    )(*rows, key_weight, value_weight)
    terms = [swapped(term, by + 1) for by, term in enumerate(terms)]
    fresh, *outgoing = call(
        functools.partial(
            fresh_body, seq_size, text_rows, local_kv, head_size, score_scale, block_keys
        ),
        (sds((kv_blocks * new_rows, head_depth), bf16),)
        + (sds(message.shape, bf16),) * seq_size,
        attend_flops * new_rows // cached_rows,
        8 * every_row * kv_width,
        2 * seq_size + 3,
    )(own_term, key_gain.reshape(1, head_depth), *terms, *messages, *cached)
    made = fresh.reshape(2, local_kv, new_rows, head_depth)
    new_keys, new_values = (jnp.swapaxes(part, 0, 1) for part in made)
    crossed = [outgoing[0]] + [swapped(outgoing[by], by) for by in range(1, seq_size)]
    attended = call(
        functools.partial(merge_body, seq_size, text_rows),
        sds((text_rows, local_heads * head_depth), bf16),
        seq_size * query_rows * head_depth,
        2 * seq_size * query_rows * head_depth,
        seq_size,
    )(*crossed)
    every = [attended] + [swapped(attended, by) for by in range(1, seq_size)]

    all_rows = seq_size * text_rows
    out_width = out_weight.shape[1]
    out_rows = all_rows // (section_size * head_size)
    sent, kept = call(
        functools.partial(output_body, seq_size, head_size, section_size),
        (
            sds(((head_size - 1) * section_size * out_rows, out_width), bf16),
            sds((section_size * out_rows, out_width), f32),
        ),
        2 * all_rows * out_weight.size,
        2 * out_weight.size,
        seq_size + 1,
        scratch=[
            pltpu.VMEM((all_rows, local_heads * head_depth), f32),
            pltpu.VMEM((all_rows, out_width), f32),
        ],
        limit=24 << 20,
    )(
        *every,
        out_weight,
    )
    sent = sent.reshape(head_size - 1, section_size * out_rows, out_width)
    got = [shifted(sent[by - 1], "head", by) for by in range(1, head_size)]
    sent, own_rows = call(
        functools.partial(turn_body, section_size),
        (
            sds(((section_size - 1) * out_rows, out_width), bf16),
            sds((out_rows, out_width), f32),
        ),
        kept.size,
        8 * kept.size,
        head_size,
        scratch=[pltpu.VMEM(kept.shape, f32)],
    )(kept, *got)
    sent = sent.reshape(section_size - 1, out_rows, out_width)
    for by in range(1, section_size):
        own_rows = own_rows + shifted(sent[by - 1], "section", by).astype(f32)
    return (own_rows.astype(bf16), new_keys, new_values)


def solution(mesh):
    placed = (
        P(("groups", "seq"), ("section", "head"), None),
        P(("groups", "seq"), ("section", "head"), None),
        P(("groups", "seq"), ("section", "head"), None),
        P(("groups", "seq"), None),
        P("seq", ("section", "head")),
        P("seq", ("section", "head")),
        P(),
        P(("section", "head"), "seq"),
        P("groups"),
        P(("groups", "seq")),
    )
    return jax.shard_map(
        on_device,
        mesh=mesh,
        in_specs=placed,
        out_specs=(
            P(("groups", "section", "head"), "seq"),
            P(("groups", "seq"), ("section", "head"), None),
            P(("groups", "seq"), ("section", "head"), None),
        ),
        check_vma=False,
    )
```
